128 devices in a mesh: grp: 16 (over x, z_hi, core), seq: 8 (over y, z_lo).
Axes of the slice: x: 4, y: 4, z: 4 (z_hi: 2, z_lo: 2; z = z_hi * 2 + z_lo), core: 2. Of those that a mesh axis runs over, the one named last changes fastest.
Arguments:
- lengths: int32 [32], replicated, may hold values from 64 to 2048, as said below
- group_of: int32 [32], replicated, may hold values from 0 to 15, as said below
- query_pre: bfloat16 [32768, 8192], P(('grp', 'seq')), may hold values from -170 to 170
- key_pre: bfloat16 [32768, 1024], P(('grp', 'seq')), may hold values from -7 to 7
- value_pre: bfloat16 [32768, 1024], P(('grp', 'seq')), may hold values from -4 to 4
- query_new: bfloat16 [32, 8192], P(None, 'seq'), may hold values from -170 to 170
- key_new: bfloat16 [32, 1024], P(None, 'seq'), may hold values from -4 to 4
- value_new: bfloat16 [32, 1024], P(None, 'seq'), may hold values from -4 to 4
- hidden_new: bfloat16 [32, 8192], P(None, 'grp'), may hold values from -3 to 3
- out_weight: bfloat16 [8192, 8192], P('seq', 'grp'), may hold values from -0.0625 to 0.0625
- norm_gain: bfloat16 [8192], P('grp'), may hold values from 0.099609375 to 1.8984375
- gate_weight: bfloat16 [8192, 16384], P('grp', 'seq'), may hold values from -0.0625 to 0.0625
- up_weight: bfloat16 [8192, 16384], P('grp', 'seq'), may hold values from -0.0625 to 0.0625
- down_weight: bfloat16 [16384, 8192], P('seq', 'grp'), may hold values from -0.046875 to 0.046875
Outputs:
- prefill_attention: bfloat16 [32768, 8192], P(('grp', 'seq'))
- decode_hidden: bfloat16 [32, 8192], P(None, ('grp', 'seq'))
The draws below stay inside these ranges and needn't reach their ends.
Inputs may be any that keep to these rules, and one draw needn't show every extreme that they name: Two requests have length exactly 2048 and are alone in their groups; the others have lengths from 64 to 512; the lengths in one group sum to at most 2048. `group_of`: every group holds at least one request and at most three.
All inputs are finite; a program needn't handle non-finite values.
Results may differ from the reference program's by a relative error of at most 0.0095.
Values may be sent and summed in bfloat16 or wider, within the bound.
A program may use at most 320 MiB of HBM per device.

```python
import math
import jax
import jax.numpy as jnp
from jax import lax

D = 8192
H = 64
KVH = 8
HD = 128
FF_WIN = 16384
GROUPS = 16
G_TOK = 2048
TOKENS = 32768
REQS = 32
SHORT_MAX = 512


def request_plan(key):
    key_groups = jax.random.fold_in(key, 101)
    key_order = jax.random.fold_in(key, 102)
    key_length = jax.random.fold_in(key, 103)
    groups = jax.random.permutation(key_groups, GROUPS).astype(jnp.int32)
    order = jax.random.permutation(key_order, REQS).astype(jnp.int32)
    ranks = jnp.zeros((REQS,), jnp.int32).at[order].set(jnp.arange(REQS, dtype=jnp.int32))
    short_rank = jnp.maximum(ranks - 2, 0)
    long_group = groups[jnp.minimum(ranks, 1)]
    short_group = groups[2 + jnp.mod(short_rank, GROUPS - 2)]
    group_of = jnp.where(ranks < 2, long_group, short_group).astype(jnp.int32)
    short_len = jax.random.randint(key_length, (REQS,), SHORT_MAX // 8, SHORT_MAX + 1).astype(jnp.int32)
    lengths = jnp.where(ranks < 2, G_TOK, short_len).astype(jnp.int32)
    return (lengths, group_of)


def draw_lengths(key, part):
    return request_plan(key)[0]


def draw_group_of(key, part):
    return request_plan(key)[1]


def attention_rows(key):
    key_query = jax.random.fold_in(key, 201)
    key_key = jax.random.fold_in(key, 202)
    keys = jax.random.truncated_normal(key_key, -6.0, 6.0, (TOKENS, KVH * HD), jnp.float32)
    queries = jax.random.truncated_normal(key_query, -6.0, 6.0, (TOKENS, H * HD), jnp.float32)
    return (queries, keys)


def draw_query_pre(key, part):
    return attention_rows(key)[0].astype(jnp.bfloat16)


def draw_key_pre(key, part):
    return attention_rows(key)[1].astype(jnp.bfloat16)


def draw_query_new(key, part):
    key_query = jax.random.fold_in(key, 301)
    queries = jax.random.truncated_normal(key_query, -6.0, 6.0, (REQS, H * HD), jnp.float32)
    return queries.astype(jnp.bfloat16)


def levels(key, shape, split, least, high):
    level = 1.0
    for dim, shards_of in split:
        heights = jax.random.uniform(jax.random.fold_in(jax.random.fold_in(key, 6), dim), (shards_of,), jnp.float32, least / len(split), high / len(split))
        level = level * jnp.repeat(jnp.exp(heights), shape[dim] // shards_of).reshape((-1,) + (1,) * (len(shape) - 1 - dim))
    return level


def bell_draw(key, dims, width, most, cuts=(), kind=jnp.bfloat16):
    level = levels(key, dims, cuts, -0.22, 0.18) if cuts else 1.0
    values = jax.random.normal(key, dims, jnp.float32) * width * level
    return jnp.minimum(jnp.maximum(values, -most), most).astype(kind)


def setup_inputs(seed: int = 0) -> dict:
    seeds = jax.random.split(jax.random.key(seed), 15)
    lengths = draw_lengths(jax.random.fold_in(seeds[14], 71), 0)
    group_of = draw_group_of(jax.random.fold_in(seeds[14], 71), 0)
    query_pre = draw_query_pre(jax.random.fold_in(seeds[14], 71), 0)
    key_pre = draw_key_pre(jax.random.fold_in(seeds[14], 71), 0)
    value_pre = bell_draw(seeds[4], (TOKENS, KVH * HD), 1.0, 4.0, ((0, 128),))
    query_new = draw_query_new(jax.random.fold_in(seeds[14], 71), 0)
    key_new = bell_draw(seeds[6], (REQS, KVH * HD), 1.0, 4.0, ((1, 8),))
    value_new = bell_draw(seeds[7], (REQS, KVH * HD), 1.0, 4.0, ((1, 8),))
    hidden_new = bell_draw(seeds[8], (REQS, D), 0.5, 3.0, ((1, 16),))
    out_weight = bell_draw(seeds[9], (H * HD, D), (H * HD) ** -0.5, 0.0625, ((0, 8), (1, 16)))
    norm_gain = jnp.clip(1.0 + 0.18 * jax.random.normal(seeds[10], (D,), jnp.float32), 0.099609375, 1.8984375).astype(jnp.bfloat16)
    gate_weight = bell_draw(seeds[11], (D, FF_WIN), D ** -0.5, 0.0625, ((0, 16), (1, 8)))
    up_weight = bell_draw(seeds[12], (D, FF_WIN), D ** -0.5, 0.0625, ((0, 16), (1, 8)))
    down_weight = bell_draw(seeds[13], (FF_WIN, D), FF_WIN ** -0.5, 0.046875, ((0, 8), (1, 16)))
    return {"lengths": lengths, "group_of": group_of, "query_pre": query_pre, "key_pre": key_pre, "value_pre": value_pre, "query_new": query_new, "key_new": key_new, "value_new": value_new, "hidden_new": hidden_new, "out_weight": out_weight, "norm_gain": norm_gain, "gate_weight": gate_weight, "up_weight": up_weight, "down_weight": down_weight}


NEGATIVE = -1e+30

def request_starts(lengths, group_of):
    index = jnp.arange(lengths.shape[0], dtype=jnp.int32)
    same = group_of[None, :] == group_of[:, None]
    before = index[None, :] < index[:, None]
    return lax.optimization_barrier(jnp.sum(jnp.where(same & before, lengths[None, :], 0), axis=1)).astype(jnp.int32)

def slot_owner(group_idx, starts, lengths, group_of, first, count):
    slots = first + jnp.arange(count, dtype=jnp.int32)
    inside = (group_of[None, :] == group_idx) & (slots[:, None] >= starts[None, :]) & (slots[:, None] < (starts + lengths)[None, :])
    labels = jnp.arange(lengths.shape[0], dtype=jnp.int32) + 1
    return (lax.optimization_barrier(jnp.sum(jnp.where(inside, labels[None, :], 0), axis=1)) - 1).astype(jnp.int32)

def reference(lengths, group_of, query_pre, key_pre, value_pre, query_new, key_new, value_new, hidden_new, out_weight, norm_gain, gate_weight, up_weight, down_weight):
    scale = 1.0 / math.sqrt(HD)
    grouped = H // KVH
    block = min(512, G_TOK)
    starts = request_starts(lengths, group_of)
    query_groups = query_pre.reshape(GROUPS, G_TOK, KVH, grouped, HD)
    key_groups = key_pre.reshape(GROUPS, G_TOK, KVH, HD)
    value_groups = value_pre.reshape(GROUPS, G_TOK, KVH, HD)

    def one_group(packed):
        group_idx, queries, keys, values = packed
        owners = slot_owner(group_idx, starts, lengths, group_of, 0, G_TOK)
        keys_wide = keys.astype(jnp.float32)
        values_wide = values.astype(jnp.float32)
        columns = jnp.arange(G_TOK, dtype=jnp.int32)

        def one_block(block_idx):
            first = (block_idx * block).astype(jnp.int32)
            rows_q = lax.dynamic_slice_in_dim(queries, first, block, 0).astype(jnp.float32)
            owner_rows = lax.dynamic_slice_in_dim(owners, first, block, 0)
            rows = first + jnp.arange(block, dtype=jnp.int32)
            scores = jnp.einsum('qkgd,tkd->kgqt', rows_q, keys_wide) * scale
            allowed = (owner_rows[:, None] == owners[None, :]) & (owner_rows[:, None] >= 0) & (columns[None, :] <= rows[:, None])
            scores = jnp.where(allowed[None, None], scores, NEGATIVE)
            top = lax.optimization_barrier(jnp.max(scores, axis=-1, keepdims=True))
            weights = jnp.where(allowed[None, None], jnp.exp(scores - top), 0.0)
            total = lax.optimization_barrier(jnp.sum(weights, axis=-1))
            rounded = weights.astype(jnp.bfloat16).astype(jnp.float32)
            mixed = jnp.einsum('kgqt,tkd->qkgd', rounded, values_wide)
            live = owner_rows >= 0
            denom = jnp.where(live[None, None, :], total, 1.0)
            result = mixed / jnp.transpose(denom, (2, 0, 1))[..., None]
            result = jnp.where(live[:, None, None, None], result, 0.0)
            return result.reshape(block, H * HD).astype(jnp.bfloat16)
        outs = lax.map(one_block, jnp.arange(G_TOK // block, dtype=jnp.int32))
        return outs.reshape(G_TOK, H * HD)
    prefill = lax.map(one_group, (jnp.arange(GROUPS, dtype=jnp.int32), query_groups, key_groups, value_groups))
    prefill_attention = prefill.reshape(TOKENS, H * HD)

    def one_request(request):
        group_idx = group_of[request]
        owners = slot_owner(group_idx, starts, lengths, group_of, 0, G_TOK)
        keys = key_groups[group_idx].astype(jnp.float32)
        values = value_groups[group_idx].astype(jnp.float32)
        query = query_new[request].reshape(KVH, grouped, HD).astype(jnp.float32)
        own_key = key_new[request].reshape(KVH, HD).astype(jnp.float32)
        own_value = value_new[request].reshape(KVH, HD).astype(jnp.float32)
        scores = jnp.einsum('kgd,tkd->kgt', query, keys) * scale
        own = jnp.einsum('kgd,kd->kg', query, own_key) * scale
        match = owners == request
        scores = jnp.where(match[None, None, :], scores, NEGATIVE)
        top = jnp.maximum(lax.optimization_barrier(jnp.max(scores, axis=-1)), own)
        weights = jnp.where(match[None, None, :], jnp.exp(scores - top[..., None]), 0.0)
        own_weight = jnp.exp(own - top)
        total = lax.optimization_barrier(jnp.sum(weights, axis=-1)) + own_weight
        mixed = jnp.einsum('kgt,tkd->kgd', weights.astype(jnp.bfloat16).astype(jnp.float32), values)
        mixed = mixed + own_weight.astype(jnp.bfloat16).astype(jnp.float32)[..., None] * own_value[:, None, :]
        return (mixed / total[..., None]).reshape(H * HD).astype(jnp.bfloat16)
    decode_att = lax.map(one_request, jnp.arange(REQS, dtype=jnp.int32))
    resid = hidden_new.astype(jnp.float32) + jnp.dot(decode_att, out_weight, preferred_element_type=jnp.float32)
    squares = lax.optimization_barrier(jnp.sum(resid * resid, axis=-1, keepdims=True))
    normed = (resid * lax.rsqrt(squares / D + 1e-05) * norm_gain.astype(jnp.float32)[None, :]).astype(jnp.bfloat16)
    gate = jnp.dot(normed, gate_weight, preferred_element_type=jnp.float32)
    upper = jnp.dot(normed, up_weight, preferred_element_type=jnp.float32)
    hidden = (jax.nn.silu(gate) * upper).astype(jnp.bfloat16)
    decode_hidden = (resid + jnp.dot(hidden, down_weight, preferred_element_type=jnp.float32)).astype(jnp.bfloat16)
    return (prefill_attention, decode_hidden)
```

```python
import functools
import math

import jax
import jax.numpy as jnp
from jax import lax
from jax.experimental import pallas as pl
from jax.experimental.pallas import tpu as pltpu
from jax.sharding import PartitionSpec as P

HD = 128
SEQ = 8
GRP = 16
ROWS = 256
KVH = 8
GROUPED = 8
REQS = 32
D = 8192
SCALE = 1.0 / math.sqrt(HD)
LOG2E = math.log2(math.e)
NEGATIVE = -1e30
FAR = -float(2**23)
F32 = jnp.float32
BF16 = jnp.bfloat16
NT = (((1,), (1,)), ((), ()))


def iota(shape, dim):
    return lax.broadcasted_iota(jnp.int32, shape, dim)


def as_column(row, count):
    eye = iota((count, 128), 0) == iota((count, 128), 1)
    return jnp.sum(jnp.where(eye, row, 0), axis=1, keepdims=True)


def request_tables(meta_ref):
    lengths = meta_ref[0:1, :]
    groups = meta_ref[1:2, :]
    len_col = as_column(lengths, 128)
    grp_col = as_column(groups, 128)
    before = (grp_col == groups) & (iota((128, 128), 0) < iota((128, 128), 1))
    starts = jnp.sum(jnp.where(before, len_col, 0), axis=0, keepdims=True)
    ranks = jnp.sum(jnp.where(before, 1, 0), axis=0, keepdims=True)
    return lengths, groups, starts, ranks


def owner_onehot(tables, group, first, count):
    lengths, groups, starts, _ = tables
    slot = first + iota((count, 128), 0)
    return (groups == group) & (slot >= starts) & (slot < starts + lengths)


def attend_kernel(meta_ref, q_ref, kv_ref, o_ref, qx, kx, top, total, accum, low):
    head = pl.program_id(0)
    seq = lax.axis_index("seq")
    group = lax.axis_index("grp")

    @pl.when(head == 0)
    def _():
        tables = request_tables(meta_ref)
        lengths, groups, starts, _ = tables
        lane = iota((ROWS, 128), 1)
        rows_in = owner_onehot(tables, group, seq * ROWS, ROWS)
        qx[...] = jnp.where(((lane < REQS) & ~rows_in) | (lane == 127), FAR, 0.0).astype(BF16)
        for part in range(SEQ):
            cols_in = owner_onehot(tables, group, part * ROWS, ROWS)
            none = jnp.sum(jnp.where(cols_in, 1.0, 0.0), axis=1, keepdims=True) == 0.0
            kx[part * ROWS : (part + 1) * ROWS, :] = jnp.where(cols_in | (none & (lane == 127)), 1.0, 0.0).astype(BF16)
        first = seq * ROWS
        touches = (groups == group) & (starts < first + ROWS) & (starts + lengths > first)
        low[0] = jnp.min(jnp.where(touches, starts, 4096))

    for a in range(GROUPED):
        top[a] = jnp.full((ROWS, 128), NEGATIVE, F32)
        total[a] = jnp.zeros((ROWS, 128), F32)
        accum[a] = jnp.zeros((ROWS, 128), F32)

    def block(j, diagonal):
        keys = kv_ref[pl.ds(2 * j, 2), 0, 0].reshape(512, HD)
        values = kv_ref[pl.ds(2 * j, 2), 0, 1].reshape(512, HD)
        keys = jnp.concatenate([keys, kx[pl.ds(pl.multiple_of(j * 512, 512), 512), :]], 1)
        if diagonal:
            causal = (j * 512 + iota((ROWS, 512), 1)) <= (seq * ROWS + iota((ROWS, 512), 0))
        scores = []
        for a in range(GROUPED):
            queries = jnp.concatenate([q_ref[:, a * HD : (a + 1) * HD], qx[...]], 1)
            scores.append(lax.dot_general(queries, keys, NT, preferred_element_type=F32))
        for a in range(GROUPED):
            s = scores[a]
            if diagonal:
                s = jnp.where(causal, s, NEGATIVE)
            old = top[a]
            m = s[:, 0:128]
            for i in range(1, 4):
                m = jnp.maximum(m, s[:, i * 128 : (i + 1) * 128])
            new = jnp.maximum(old, jnp.max(m, axis=1, keepdims=True))
            decay = jnp.exp2((old - new) * (SCALE * LOG2E))
            shift = new * (SCALE * LOG2E)
            p = jnp.concatenate(
                [jnp.exp2(s[:, i * 128 : (i + 1) * 128] * (SCALE * LOG2E) - shift) for i in range(4)], 1
            )
            t = p[:, 0:128]
            for i in range(1, 4):
                t = t + p[:, i * 128 : (i + 1) * 128]
            total[a] = total[a] * decay + t
            top[a] = new
            accum[a] = accum[a] * decay + jnp.dot(p.astype(BF16), values, preferred_element_type=F32)

    last = seq // 2
    begin = low[0] // 512

    @pl.when(begin <= last)
    def _():
        def step(j, carry):
            block(j, False)
            return carry

        lax.fori_loop(begin, last, step, 0)
        block(last, True)

    live = jnp.min(qx[...].astype(F32)[:, 0:128] * jnp.where(iota((ROWS, 128), 1) < REQS, 1.0, 0.0), axis=1, keepdims=True)
    held = jnp.sum(jnp.where((iota((ROWS, 128), 1) < REQS) & (qx[...].astype(F32) == 0.0), 1.0, 0.0), axis=1, keepdims=True)
    del live
    for a in range(GROUPED):
        t = jnp.sum(total[a], axis=1, keepdims=True)
        out = jnp.where(held > 0.0, accum[a] / jnp.where(held > 0.0, t, 1.0), 0.0)
        o_ref[:, a * HD : (a + 1) * HD] = out.astype(BF16)


def attend(meta, queries, kvg):
    return pl.pallas_call(
        attend_kernel,
        grid=(KVH,),
        out_shape=jax.ShapeDtypeStruct((ROWS, D), BF16),
        in_specs=[
            pl.BlockSpec((8, 128), lambda h: (0, 0)),
            pl.BlockSpec((ROWS, GROUPED * HD), lambda h: (0, h)),
            pl.BlockSpec((SEQ, 1, 2, ROWS, HD), lambda h: (0, h, 0, 0, 0)),
        ],
        out_specs=pl.BlockSpec((ROWS, GROUPED * HD), lambda h: (0, h)),
        scratch_shapes=[
            pltpu.VMEM((ROWS, 128), BF16),
            pltpu.VMEM((SEQ * ROWS, 128), BF16),
            pltpu.VMEM((GROUPED, ROWS, 128), F32),
            pltpu.VMEM((GROUPED, ROWS, 128), F32),
            pltpu.VMEM((GROUPED, ROWS, 128), F32),
            pltpu.SMEM((1,), jnp.int32),
        ],
        compiler_params=pltpu.CompilerParams(vmem_limit_bytes=50 << 20),
        cost_estimate=pl.CostEstimate(flops=17 << 30, bytes_accessed=16 << 20, transcendentals=32 << 20),
        name="attend",
    )(meta, queries, kvg)


def remote(src, dst, send_sem, recv_sem, device):
    return pltpu.make_async_remote_copy(src_ref=src, dst_ref=dst, send_sem=send_sem, recv_sem=recv_sem, device_id=device)


class Exchange:
    def __init__(self, axis, count, me, source, landing, send_sem, recv_sem, spread=lambda i: i):
        self.axis, self.count, self.me, self.spread = axis, count, me, spread
        self.source, self.landing, self.send_sem, self.recv_sem = source, landing, send_sem, recv_sem

    def start(self):
        for i in range(1, self.count):
            peer = (self.me + i) % self.count
            remote(
                self.source(peer),
                self.landing.at[self.me],
                self.send_sem.at[i],
                self.recv_sem.at[self.me],
                {self.axis: self.spread(peer)},
            ).start()

    def wait(self):
        for i in range(1, self.count):
            peer = (self.me + i) % self.count
            copy = remote(
                self.source(peer),
                self.landing.at[peer],
                self.send_sem.at[i],
                self.recv_sem.at[peer],
                {self.axis: self.spread(peer)},
            )
            copy.wait_send()
            copy.wait_recv()


def step_kernel(
    meta_ref, k_ref, v_ref, qn_ref, kn_ref, vn_ref, hid_ref, gain_ref, ow_ref, gw_ref, uw_ref, dw_ref,
    kvg, dec_ref,
    owb, gwb, uwb, dwb, qmsg, qall, pmsg, part, amsg, aall, pblk, prs, rmsg, rall, gmsg, grs, hmsg, hall, dblk, drs,
    wsem, lsem, kss, krs, qss, qrs, pss, prsem, ass, ars, oss, ors, rss, rrs, gss, grsem, hss, hrs, dss, drsem,
):
    seq = lax.axis_index("seq")
    group = lax.axis_index("grp")
    y, z = seq // 2, seq % 2
    pair = seq + 1 - 2 * z
    up, down = (seq + 2) % SEQ, (seq + 6) % SEQ

    barrier = pltpu.get_barrier_semaphore()
    for i in range(1, SEQ):
        pl.semaphore_signal(barrier, inc=1, device_id={"seq": (seq + i) % SEQ})
    for i in range(1, GRP):
        pl.semaphore_signal(barrier, inc=1, device_id={"grp": (group + i) % GRP})

    def own_copy(h, which):
        src = (k_ref, v_ref)[which].at[:, pl.ds(pl.multiple_of(h * HD, HD), HD)]
        return pltpu.make_async_copy(src, kvg.at[seq, h, which], lsem.at[h, which])

    def own_start(h, carry):
        own_copy(h, 0).start()
        own_copy(h, 1).start()
        return carry

    lax.fori_loop(0, KVH, own_start, 0)
    weights = [(ow_ref, owb), (gw_ref, gwb), (uw_ref, uwb), (dw_ref, dwb)]
    for i, (src, dst) in enumerate(weights):
        pltpu.make_async_copy(src, dst, wsem.at[i]).start()

    def weight_wait(i):
        pltpu.make_async_copy(weights[i][0], weights[i][1], wsem.at[i]).wait()

    lengths, groups, starts, ranks = request_tables(meta_ref)
    slot32 = iota((REQS, 128), 0) % 4
    pick = (groups == group) & (ranks == slot32)
    pick32 = jnp.where(pick, 1.0, 0.0).astype(BF16)[:, 0:REQS]
    block32 = iota((REQS, HD), 0) // 4
    spread_q = jnp.dot(pick32, qn_ref[...], preferred_element_type=F32)
    mine_q = jnp.zeros((REQS, HD), F32)
    for a in range(GROUPED):
        mine_q = mine_q + jnp.where(block32 == a, spread_q[:, a * HD : (a + 1) * HD], 0.0)
    qmsg[...] = mine_q.astype(BF16)
    qall[seq] = mine_q.astype(BF16)

    pl.semaphore_wait(barrier, SEQ + GRP - 2)

    ex_q = Exchange("seq", SEQ, seq, lambda p: qmsg, qall, qss, qrs)
    ex_p = Exchange("seq", SEQ, seq, lambda p: pmsg.at[p], part, pss, prsem)
    ex_a = Exchange("grp", GRP, group, lambda p: amsg, aall, ass, ars)
    ex_o = Exchange("seq", SEQ, seq, lambda p: pblk.at[p // 2], prs, oss, ors)
    ex_r = Exchange("seq", 4, y, lambda p: rmsg, rall, rss, rrs, lambda p: 2 * p + z)
    ex_g = Exchange("grp", GRP, group, lambda p: gmsg.at[p], grs, gss, grsem)
    ex_h = Exchange("grp", GRP, group, lambda p: hmsg, hall, hss, hrs)
    ex_d = Exchange("seq", SEQ, seq, lambda p: dblk.at[p // 2], drs, dss, drsem)

    def relay(h, slot, shard, dst):
        return remote(kvg.at[shard, h], kvg.at[shard, h], kss.at[h, slot], krs.at[shard, h], {"seq": dst})

    turn = ((y + 1) // 2 + 1) % 2
    cross = 2 * (1 - y % 2) + z
    far = (seq + 4) % SEQ

    def sends(h):
        return [
            (0, seq, pair, y >= 0),
            (1, seq, up, y < 3),
            (2, seq, down, (y == 0) | ((y == 1) & (h % 2 == 1))),
            (3, pair, up, y < 3),
            (4, pair, down, y == 0),
            (5, cross, (seq + 2 + 4 * turn) % SEQ, h % 2 == turn),
            (6, far, pair, y >= 2),
        ]

    def start(h, slots):
        for slot, shard, dst, on in sends(h):
            if slot in slots:

                @pl.when(on)
                def _():
                    relay(h, slot, shard, dst).start()

    def arrived(h, shard):
        relay(h, 0, shard, pair).wait_recv()

    def relay_first(h):
        own_copy(h, 0).wait()
        own_copy(h, 1).wait()
        start(h, (0, 1, 2))

    def relay_second(h):
        arrived(h, pair)
        start(h, (3, 4))

        @pl.when(h % 2 == turn)
        def _():
            arrived(h, cross)

        start(h, (5,))

    def relay_third(h):
        @pl.when(y >= 2)
        def _():
            arrived(h, far)

        start(h, (6,))

    def relay_last(h):
        for t in range(SEQ):
            seen = ((t == cross) & (h % 2 == turn)) | ((t == far) & (y >= 2))

            @pl.when((t // 2 < y) & jnp.logical_not(seen))
            def _():
                arrived(h, t)

    def relay_sent(h):
        for slot, shard, dst, on in sends(h):

            @pl.when(on)
            def _():
                relay(h, slot, shard, dst).wait_send()

    def dec0():
        ex_q.start()

    def dec1():
        ex_q.wait()
        start_c = jnp.sum(jnp.where(pick, starts, 0), axis=1, keepdims=True)
        len_c = jnp.sum(jnp.where(pick, lengths, 0), axis=1, keepdims=True)
        pos = seq * ROWS + iota((REQS, ROWS), 1)
        allowed = (pos >= start_c) & (pos < start_c + len_c)
        for t in range(SEQ):
            s = lax.dot_general(qall[t], k_ref[:, t * HD : (t + 1) * HD], NT, preferred_element_type=F32) * SCALE
            s = jnp.where(allowed, s, NEGATIVE)
            m = jnp.max(s, axis=1, keepdims=True)
            p = jnp.where(allowed, jnp.exp(s - m), 0.0)
            l = jnp.sum(p, axis=1, keepdims=True)
            pmsg[t, 0] = jnp.dot(p.astype(BF16), v_ref[:, t * HD : (t + 1) * HD], preferred_element_type=F32)
            pmsg[t, 1] = jnp.where(iota((REQS, HD), 1) == 0, m, l)
        part[seq] = pmsg[seq]
        ex_p.start()

    def dec2():
        ex_p.wait()
        key_row = jnp.dot(pick32, kn_ref[...], preferred_element_type=F32)
        value_row = jnp.dot(pick32, vn_ref[...], preferred_element_type=F32)
        own = jnp.sum(qmsg[...].astype(F32) * key_row, axis=1, keepdims=True) * SCALE
        top = own
        for t in range(SEQ):
            top = jnp.maximum(top, part[t, 1][:, 0:1])
        weight = jnp.exp(own - top)
        total = weight
        mixed = weight.astype(BF16).astype(F32) * value_row
        for t in range(SEQ):
            scale = jnp.exp(part[t, 1][:, 0:1] - top)
            total = total + scale * part[t, 1][:, 1:2]
            mixed = mixed + scale * part[t, 0]
        out = (mixed / total).astype(BF16)
        amsg[...] = out
        aall[group] = out
        ex_a.start()

    def dec3():
        ex_a.wait()
        rank_col = as_column(ranks, REQS)
        grp_col = as_column(groups, REQS)
        target = jnp.concatenate([grp_col * 32 + a * 4 + rank_col for a in range(GROUPED)], 0)
        gather = jnp.where(iota((256, 512), 1) == target, 1.0, 0.0).astype(BF16)
        rows = jnp.dot(gather, aall[...].reshape(512, HD), preferred_element_type=F32).astype(BF16)
        att = jnp.concatenate([rows[a * 32 : (a + 1) * 32] for a in range(GROUPED)], 1)
        weight_wait(0)
        proj = jnp.dot(att, owb[...], preferred_element_type=F32)
        for b in range(4):
            pblk[b] = proj[:, b * 128 : (b + 1) * 128]
        prs[seq] = pblk[y]
        ex_o.start()

    def dec4():
        ex_o.wait()
        r = hid_ref[:, pl.ds(pl.multiple_of(y * 128, 128), 128)].astype(F32)
        for t in range(SEQ):
            r = r + prs[t]
        rmsg[...] = r
        rall[y] = r
        ex_r.start()

    def dec5():
        ex_r.wait()
        r = jnp.concatenate([rall[b] for b in range(4)], 1)
        squares = jnp.sum(r * r, axis=1, keepdims=True)
        x = (r * gain_ref[...].astype(F32)).astype(BF16)
        eye = iota((REQS, 128), 0) == iota((REQS, 128), 1)
        row = jnp.sum(jnp.where(eye, squares, 0.0), axis=0, keepdims=True)
        weight_wait(1)
        weight_wait(2)
        gate = jnp.dot(x, gwb[...], preferred_element_type=F32)
        upper = jnp.dot(x, uwb[...], preferred_element_type=F32)
        for t in range(GRP):
            gmsg[t, 0:32] = gate[:, t * 128 : (t + 1) * 128]
            gmsg[t, 32:64] = upper[:, t * 128 : (t + 1) * 128]
            gmsg[t, 64:72] = jnp.broadcast_to(row, (8, 128))
        grs[group] = gmsg[group]
        ex_g.start()

    def dec6():
        ex_g.wait()
        acc = grs[0]
        for t in range(1, GRP):
            acc = acc + grs[t]
        squares = as_column(acc[64:65, :], REQS)
        r = lax.rsqrt(squares / D + 1e-05)
        gate = acc[0:32] * r
        upper = acc[32:64] * r
        out = (gate / (1.0 + jnp.exp(-gate)) * upper).astype(BF16)
        hmsg[...] = out
        hall[group] = out
        ex_h.start()

    def dec7():
        ex_h.wait()
        hidden = jnp.concatenate([hall[t] for t in range(GRP)], 1)
        weight_wait(3)
        out = jnp.dot(hidden, dwb[...], preferred_element_type=F32)
        for b in range(4):
            dblk[b] = out[:, b * 128 : (b + 1) * 128]
        drs[seq] = dblk[y]
        ex_d.start()

    def dec8():
        ex_d.wait()
        out = rmsg[...]
        for t in range(SEQ):
            out = out + drs[t]
        dec_ref[...] = jnp.where(z == 0, out[:, 0:64], out[:, 64:128]).astype(BF16)

    steps = [dec0, dec1, dec2, dec3, dec4, dec5, dec6, dec7, dec8]

    def turn_body(it, carry):
        @pl.when(it < KVH)
        def _():
            relay_first(it)

        for i, dec in enumerate(steps):
            pl.when(it == i)(dec)

        @pl.when((it >= 1) & (it <= KVH))
        def _():
            relay_second(it - 1)

        @pl.when(it >= 2)
        def _():
            relay_third(it - 2)

        return carry

    lax.fori_loop(0, KVH + 2, turn_body, 0)

    def drain(h, carry):
        relay_last(h)
        relay_sent(h)
        return carry

    lax.fori_loop(0, KVH, drain, 0)


def step(meta, k, v, qn, kn, vn, hid, gain, ow, gw, uw, dw):
    vmem = pl.BlockSpec(memory_space=pltpu.VMEM)
    hbm = pl.BlockSpec(memory_space=pl.ANY)
    dma = pltpu.SemaphoreType.DMA
    return pl.pallas_call(
        step_kernel,
        out_shape=(
            jax.ShapeDtypeStruct((SEQ, KVH, 2, ROWS, HD), BF16),
            jax.ShapeDtypeStruct((REQS, 64), BF16),
        ),
        in_specs=[vmem] * 8 + [hbm] * 4,
        out_specs=(hbm, vmem),
        scratch_shapes=[
            pltpu.VMEM((1024, 512), BF16),
            pltpu.VMEM((512, 2048), BF16),
            pltpu.VMEM((512, 2048), BF16),
            pltpu.VMEM((2048, 512), BF16),
            pltpu.VMEM((32, 128), BF16),
            pltpu.VMEM((8, 32, 128), BF16),
            pltpu.VMEM((8, 2, 32, 128), F32),
            pltpu.VMEM((8, 2, 32, 128), F32),
            pltpu.VMEM((32, 128), BF16),
            pltpu.VMEM((16, 32, 128), BF16),
            pltpu.VMEM((4, 32, 128), F32),
            pltpu.VMEM((8, 32, 128), F32),
            pltpu.VMEM((32, 128), F32),
            pltpu.VMEM((4, 32, 128), F32),
            pltpu.VMEM((16, 72, 128), F32),
            pltpu.VMEM((16, 72, 128), F32),
            pltpu.VMEM((32, 128), BF16),
            pltpu.VMEM((16, 32, 128), BF16),
            pltpu.VMEM((4, 32, 128), F32),
            pltpu.VMEM((8, 32, 128), F32),
            dma((4,)),
            dma((8, 2)),
            dma((8, 7)),
            dma((8, 8)),
        ]
        + [dma((8,))] * 4
        + [dma((16,))] * 2
        + [dma((8,))] * 2
        + [dma((4,))] * 2
        + [dma((16,))] * 4
        + [dma((8,))] * 2,
        compiler_params=pltpu.CompilerParams(collective_id=0, has_side_effects=True, vmem_limit_bytes=40 << 20),
        name="step",
    )(meta, k, v, qn, kn, vn, hid, gain, ow, gw, uw, dw)


def shards(
    lengths, group_of, query_pre, key_pre, value_pre, query_new, key_new, value_new,
    hidden_new, out_weight, norm_gain, gate_weight, up_weight, down_weight,
):
    meta = jnp.pad(jnp.stack([lengths, group_of + 1]), ((0, 6), (0, 128 - REQS))) - jnp.array(
        [[0], [1], [0], [0], [0], [0], [0], [0]], jnp.int32
    )
    kvg, decode_hidden = step(
        meta, key_pre, value_pre, query_new, key_new, value_new, hidden_new, norm_gain.reshape(1, -1),
        out_weight, gate_weight, up_weight, down_weight,
    )
    return attend(meta, query_pre, kvg), decode_hidden


def solution(mesh):
    both = P(("grp", "seq"), None)
    return jax.shard_map(
        shards,
        mesh=mesh,
        in_specs=(
            P(), P(), both, both, both, P(None, "seq"), P(None, "seq"), P(None, "seq"), P(None, "grp"),
            P("seq", "grp"), P("grp"), P("grp", "seq"), P("grp", "seq"), P("seq", "grp"),
        ),
        out_specs=(both, P(None, ("grp", "seq"))),
        check_vma=False,
    )
```

```python
import functools
import math

import jax
import jax.numpy as jnp
from jax import lax
from jax.experimental import pallas as pl
from jax.experimental.pallas import tpu as pltpu
from jax.sharding import PartitionSpec as P

HD = 128
SEQ = 8
GRP = 16
ROWS = 256
KVH = 8
GROUPED = 8
REQS = 32
D = 8192
SCALE = 1.0 / math.sqrt(HD)
LOG2E = math.log2(math.e)
NEGATIVE = -1e30
FAR = -float(2**23)
F32 = jnp.float32
BF16 = jnp.bfloat16
NT = (((1,), (1,)), ((), ()))


def iota(shape, dim):
    return lax.broadcasted_iota(jnp.int32, shape, dim)


def as_column(row, count):
    eye = iota((count, 128), 0) == iota((count, 128), 1)
    return jnp.sum(jnp.where(eye, row, 0), axis=1, keepdims=True)


def request_tables(len_ref, grp_ref):
    lengths = jnp.concatenate([len_ref[...], jnp.zeros((1, 128 - REQS), jnp.int32)], 1)
    groups = jnp.concatenate([grp_ref[...], jnp.full((1, 128 - REQS), -1, jnp.int32)], 1)
    len_col = as_column(lengths, 128)
    grp_col = as_column(groups, 128)
    before = (grp_col == groups) & (iota((128, 128), 0) < iota((128, 128), 1))
    starts = jnp.sum(jnp.where(before, len_col, 0), axis=0, keepdims=True)
    ranks = jnp.sum(jnp.where(before, 1, 0), axis=0, keepdims=True)
    return lengths, groups, starts, ranks


def owner_onehot(tables, group, first, count):
    lengths, groups, starts, _ = tables
    slot = first + iota((count, 128), 0)
    return (groups == group) & (slot >= starts) & (slot < starts + lengths)


def remote(src, dst, send_sem, recv_sem, device):
    return pltpu.make_async_remote_copy(src_ref=src, dst_ref=dst, send_sem=send_sem, recv_sem=recv_sem, device_id=device)


class Exchange:
    def __init__(self, axis, count, me, source, landing, send_sem, recv_sem, spread=lambda i: i):
        self.axis, self.count, self.me, self.spread = axis, count, me, spread
        self.source, self.landing, self.send_sem, self.recv_sem = source, landing, send_sem, recv_sem

    def start(self):
        for i in range(1, self.count):
            peer = (self.me + i) % self.count
            remote(
                self.source(peer),
                self.landing.at[self.me],
                self.send_sem.at[i],
                self.recv_sem.at[self.me],
                {self.axis: self.spread(peer)},
            ).start()

    def wait(self):
        for i in range(1, self.count):
            peer = (self.me + i) % self.count
            copy = remote(
                self.source(peer),
                self.landing.at[peer],
                self.send_sem.at[i],
                self.recv_sem.at[peer],
                {self.axis: self.spread(peer)},
            )
            copy.wait_send()
            copy.wait_recv()


def step_kernel(
    len_hbm, grp_hbm, qn_hbm, kn_hbm, vn_hbm, hid_hbm, gain_hbm, ow_ref, gw_ref, uw_ref, dw_ref, q_ref, k_ref, v_ref,
    out_ref, dec_ref,
    len_ref, grp_ref, qn_ref, kn_ref, vn_ref, hid_ref, gain_ref,
    kvg, qb, ob, qx, kx, live, top, total, accum,
    owb, gwb, uwb, dwb, qmsg, qall, pmsg, part, amsg, aall, pblk, prs, rmsg, rall, gmsg, grs, hmsg, hall, dblk, drs,
    isem, wsem, lsem, qsem, osem, kss, krs, qss, qrs, pss, prsem, ass, ars, oss, ors, rss, rrs, gss, grsem, hss, hrs, dss, drsem,
):
    seq = lax.axis_index("seq")
    group = lax.axis_index("grp")
    y, z = seq // 2, seq % 2
    pair = seq + 1 - 2 * z
    up, down = (seq + 2) % SEQ, (seq + 6) % SEQ

    barrier = pltpu.get_barrier_semaphore()
    for i in range(1, SEQ):
        pl.semaphore_signal(barrier, inc=1, device_id={"seq": (seq + i) % SEQ})
    for i in range(1, GRP):
        pl.semaphore_signal(barrier, inc=1, device_id={"grp": (group + i) % GRP})

    def own_copy(h, which):
        src = (k_ref, v_ref)[which].at[:, pl.ds(pl.multiple_of(h * HD, HD), HD)]
        return pltpu.make_async_copy(src, kvg.at[seq, h, which], lsem.at[h, which])

    def own_start(h, carry):
        own_copy(h, 0).start()
        own_copy(h, 1).start()
        return carry

    small = [
        (len_hbm, len_ref), (grp_hbm, grp_ref), (qn_hbm, qn_ref), (kn_hbm, kn_ref),
        (vn_hbm, vn_ref), (hid_hbm, hid_ref), (gain_hbm, gain_ref),
    ]
    for i, (src, dst) in enumerate(small):
        pltpu.make_async_copy(src, dst, isem.at[i]).start()
    lax.fori_loop(0, KVH, own_start, 0)

    def q_copy(h):
        cols = pl.ds(pl.multiple_of(h * 1024, 1024), 1024)
        return pltpu.make_async_copy(q_ref.at[:, cols], qb.at[:, cols], qsem.at[h])

    def out_copy(h):
        cols = pl.ds(pl.multiple_of(h * 1024, 1024), 1024)
        return pltpu.make_async_copy(ob.at[h % 2], out_ref.at[:, cols], osem.at[h % 2])

    weights = [(ow_ref, owb), (gw_ref, gwb), (uw_ref, uwb), (dw_ref, dwb)]
    for i, (src, dst) in enumerate(weights):
        pltpu.make_async_copy(src, dst, wsem.at[i]).start()

    def weight_wait(i):
        pltpu.make_async_copy(weights[i][0], weights[i][1], wsem.at[i]).wait()

    def q_start(h, carry):
        q_copy(h).start()
        return carry

    lax.fori_loop(0, KVH, q_start, 0)
    for i, (src, dst) in enumerate(small):
        pltpu.make_async_copy(src, dst, isem.at[i]).wait()

    tables = request_tables(len_ref, grp_ref)
    lengths, groups, starts, ranks = tables
    slot32 = iota((REQS, 128), 0) % 4
    pick = (groups == group) & (ranks == slot32)
    pick32 = jnp.where(pick, 1.0, 0.0).astype(BF16)[:, 0:REQS]
    block32 = iota((REQS, HD), 0) // 4
    spread_q = jnp.dot(pick32, qn_ref[...], preferred_element_type=F32)
    mine_q = jnp.zeros((REQS, HD), F32)
    for a in range(GROUPED):
        mine_q = mine_q + jnp.where(block32 == a, spread_q[:, a * HD : (a + 1) * HD], 0.0)
    qmsg[...] = mine_q.astype(BF16)
    qall[seq] = mine_q.astype(BF16)

    lane = iota((ROWS, 128), 1)
    rows_in = owner_onehot(tables, group, seq * ROWS, ROWS)
    qx[...] = jnp.where(((lane < REQS) & jnp.logical_not(rows_in)) | (lane == 127), FAR, 0.0).astype(BF16)
    held = jnp.sum(jnp.where(rows_in, 1.0, 0.0), axis=1, keepdims=True)
    live[...] = jnp.broadcast_to(held, (ROWS, 128))
    for t in range(SEQ):
        cols_in = owner_onehot(tables, group, t * ROWS, ROWS)
        none = jnp.sum(jnp.where(cols_in, 1.0, 0.0), axis=1, keepdims=True) == 0.0
        kx[t * ROWS : (t + 1) * ROWS, :] = jnp.where(cols_in | (none & (lane == 127)), 1.0, 0.0).astype(BF16)

    def own_wait(h, carry):
        own_copy(h, 0).wait()
        own_copy(h, 1).wait()
        return carry

    lax.fori_loop(0, KVH, own_wait, 0)
    pl.semaphore_wait(barrier, SEQ + GRP - 2)

    ex_q = Exchange("seq", SEQ, seq, lambda p: qmsg, qall, qss, qrs)
    ex_p = Exchange("seq", SEQ, seq, lambda p: pmsg.at[p], part, pss, prsem)
    ex_a = Exchange("grp", GRP, group, lambda p: amsg, aall, ass, ars)
    ex_o = Exchange("seq", SEQ, seq, lambda p: pblk.at[p // 2], prs, oss, ors)
    ex_r = Exchange("seq", 4, y, lambda p: rmsg, rall, rss, rrs, lambda p: 2 * p + z)
    ex_g = Exchange("grp", GRP, group, lambda p: gmsg.at[p], grs, gss, grsem)
    ex_h = Exchange("grp", GRP, group, lambda p: hmsg, hall, hss, hrs)
    ex_d = Exchange("seq", SEQ, seq, lambda p: dblk.at[p // 2], drs, dss, drsem)

    def relay(h, slot, shard, dst):
        return remote(kvg.at[shard, h], kvg.at[shard, h], kss.at[h, slot], krs.at[shard, h], {"seq": dst})

    turn = ((y + 1) // 2 + 1) % 2
    cross = 2 * (1 - y % 2) + z
    far = (seq + 4) % SEQ

    def sends(h):
        return [
            (0, seq, pair, y >= 0),
            (1, seq, up, y < 3),
            (2, seq, down, (y == 0) | ((y == 1) & (h % 2 == 1))),
            (3, pair, up, y < 3),
            (4, pair, down, y == 0),
            (5, cross, (seq + 2 + 4 * turn) % SEQ, h % 2 == turn),
            (6, far, pair, y >= 2),
        ]

    def start(h, slots):
        for slot, shard, dst, on in sends(h):
            if slot in slots:

                @pl.when(on)
                def _():
                    relay(h, slot, shard, dst).start()

    def arrived(h, shard):
        relay(h, 0, shard, pair).wait_recv()

    def relay_first(h):
        start(h, (0, 1, 2))

    def relay_second(h):
        arrived(h, pair)
        start(h, (3, 4))

        @pl.when(h % 2 == turn)
        def _():
            arrived(h, cross)

        start(h, (5,))

    def relay_third(h):
        @pl.when(y >= 2)
        def _():
            arrived(h, far)

        start(h, (6,))

    def relay_last(h):
        for t in range(SEQ):
            seen = ((t == cross) & (h % 2 == turn)) | ((t == far) & (y >= 2))

            @pl.when((t // 2 < y) & jnp.logical_not(seen))
            def _():
                arrived(h, t)

    def relay_sent(h):
        for slot, shard, dst, on in sends(h):

            @pl.when(on)
            def _():
                relay(h, slot, shard, dst).wait_send()

    def dec0():
        ex_q.start()

    def dec1():
        ex_q.wait()
        start_c = jnp.sum(jnp.where(pick, starts, 0), axis=1, keepdims=True)
        len_c = jnp.sum(jnp.where(pick, lengths, 0), axis=1, keepdims=True)
        pos = seq * ROWS + iota((REQS, ROWS), 1)
        allowed = (pos >= start_c) & (pos < start_c + len_c)
        for t in range(SEQ):
            s = lax.dot_general(qall[t], kvg[seq, t, 0], NT, preferred_element_type=F32) * SCALE
            s = jnp.where(allowed, s, NEGATIVE)
            m = jnp.max(s, axis=1, keepdims=True)
            p = jnp.where(allowed, jnp.exp(s - m), 0.0)
            l = jnp.sum(p, axis=1, keepdims=True)
            pmsg[t, 0] = jnp.dot(p.astype(BF16), kvg[seq, t, 1], preferred_element_type=F32)
            pmsg[t, 1] = jnp.where(iota((REQS, HD), 1) == 0, m, l)
        part[seq] = pmsg[seq]
        ex_p.start()

    def dec2():
        ex_p.wait()
        key_row = jnp.dot(pick32, kn_ref[...], preferred_element_type=F32)
        value_row = jnp.dot(pick32, vn_ref[...], preferred_element_type=F32)
        own = jnp.sum(qmsg[...].astype(F32) * key_row, axis=1, keepdims=True) * SCALE
        top = own
        for t in range(SEQ):
            top = jnp.maximum(top, part[t, 1][:, 0:1])
        weight = jnp.exp(own - top)
        total = weight
        mixed = weight.astype(BF16).astype(F32) * value_row
        for t in range(SEQ):
            scale = jnp.exp(part[t, 1][:, 0:1] - top)
            total = total + scale * part[t, 1][:, 1:2]
            mixed = mixed + scale * part[t, 0]
        out = (mixed / total).astype(BF16)
        amsg[...] = out
        aall[group] = out
        ex_a.start()

    def dec3():
        ex_a.wait()
        rank_col = as_column(ranks, REQS)
        grp_col = as_column(groups, REQS)
        target = jnp.concatenate([grp_col * 32 + a * 4 + rank_col for a in range(GROUPED)], 0)
        gather = jnp.where(iota((256, 512), 1) == target, 1.0, 0.0).astype(BF16)
        rows = jnp.dot(gather, aall[...].reshape(512, HD), preferred_element_type=F32).astype(BF16)
        att = jnp.concatenate([rows[a * 32 : (a + 1) * 32] for a in range(GROUPED)], 1)
        weight_wait(0)
        proj = jnp.dot(att, owb[...], preferred_element_type=F32)
        for b in range(4):
            pblk[b] = proj[:, b * 128 : (b + 1) * 128]
        prs[seq] = pblk[y]
        ex_o.start()

    def dec4():
        ex_o.wait()
        r = hid_ref[:, pl.ds(pl.multiple_of(y * 128, 128), 128)].astype(F32)
        for t in range(SEQ):
            r = r + prs[t]
        rmsg[...] = r
        rall[y] = r
        ex_r.start()

    def dec5():
        ex_r.wait()
        r = jnp.concatenate([rall[b] for b in range(4)], 1)
        squares = jnp.sum(r * r, axis=1, keepdims=True)
        x = (r * gain_ref[...].astype(F32)).astype(BF16)
        eye = iota((REQS, 128), 0) == iota((REQS, 128), 1)
        row = jnp.sum(jnp.where(eye, squares, 0.0), axis=0, keepdims=True)
        weight_wait(1)
        weight_wait(2)
        gate = jnp.dot(x, gwb[...], preferred_element_type=F32)
        upper = jnp.dot(x, uwb[...], preferred_element_type=F32)
        for t in range(GRP):
            gmsg[t, 0:32] = gate[:, t * 128 : (t + 1) * 128]
            gmsg[t, 32:64] = upper[:, t * 128 : (t + 1) * 128]
            gmsg[t, 64:72] = jnp.broadcast_to(row, (8, 128))
        grs[group] = gmsg[group]
        ex_g.start()

    def dec6():
        ex_g.wait()
        acc = grs[0]
        for t in range(1, GRP):
            acc = acc + grs[t]
        squares = as_column(acc[64:65, :], REQS)
        r = lax.rsqrt(squares / D + 1e-05)
        gate = acc[0:32] * r
        upper = acc[32:64] * r
        out = (gate / (1.0 + jnp.exp(-gate)) * upper).astype(BF16)
        hmsg[...] = out
        hall[group] = out
        ex_h.start()

    def dec7():
        ex_h.wait()
        hidden = jnp.concatenate([hall[t] for t in range(GRP)], 1)
        weight_wait(3)
        out = jnp.dot(hidden, dwb[...], preferred_element_type=F32)
        for b in range(4):
            dblk[b] = out[:, b * 128 : (b + 1) * 128]
        drs[seq] = dblk[y]
        ex_d.start()

    def dec8():
        ex_d.wait()
        out = rmsg[...]
        for t in range(SEQ):
            out = out + drs[t]
        dec_ref[...] = jnp.where(z == 0, out[:, 0:64], out[:, 64:128]).astype(BF16)

    steps = [dec0, dec1, dec2, dec3, dec4, dec5, dec6, dec7, dec8]

    def block(h, j, diagonal):
        keys = kvg[pl.ds(2 * j, 2), h, 0].reshape(512, HD)
        values = kvg[pl.ds(2 * j, 2), h, 1].reshape(512, HD)
        keys = jnp.concatenate([keys, kx[pl.ds(pl.multiple_of(j * 512, 512), 512), :]], 1)
        if diagonal:
            causal = (j * 512 + iota((ROWS, 512), 1)) <= (seq * ROWS + iota((ROWS, 512), 0))
        scores = []
        for a in range(GROUPED):
            cols = pl.ds(pl.multiple_of((h * GROUPED + a) * HD, HD), HD)
            queries = jnp.concatenate([qb[:, cols], qx[...]], 1)
            scores.append(lax.dot_general(queries, keys, NT, preferred_element_type=F32))
        for a in range(GROUPED):
            s = scores[a]
            if diagonal:
                s = jnp.where(causal, s, NEGATIVE)
            old = top[a]
            m = s[:, 0:128]
            for i in range(1, 4):
                m = jnp.maximum(m, s[:, i * 128 : (i + 1) * 128])
            new = jnp.maximum(old, jnp.max(m, axis=1, keepdims=True))
            decay = jnp.exp2((old - new) * (SCALE * LOG2E))
            shift = new * (SCALE * LOG2E)
            p = jnp.concatenate(
                [jnp.exp2(s[:, i * 128 : (i + 1) * 128] * (SCALE * LOG2E) - shift) for i in range(4)], 1
            )
            t = p[:, 0:128]
            for i in range(1, 4):
                t = t + p[:, i * 128 : (i + 1) * 128]
            total[a] = total[a] * decay + t
            top[a] = new
            accum[a] = accum[a] * decay + jnp.dot(p.astype(BF16), values, preferred_element_type=F32)

    def attend(h):
        q_copy(h).wait()
        top[...] = jnp.full((GROUPED, ROWS, 128), NEGATIVE, F32)
        total[...] = jnp.zeros((GROUPED, ROWS, 128), F32)
        accum[...] = jnp.zeros((GROUPED, ROWS, 128), F32)

        def each(j, carry):
            block(h, j, False)
            return carry

        lax.fori_loop(0, y, each, 0)
        block(h, y, True)

        @pl.when(h >= 2)
        def _():
            out_copy(h).wait()

        for a in range(GROUPED):
            t = jnp.sum(total[a], axis=1, keepdims=True)
            ok = live[...] > 0.0
            ob[h % 2, :, a * HD : (a + 1) * HD] = jnp.where(ok, accum[a] / t, 0.0).astype(BF16)
        out_copy(h).start()

    def turn_body(it, carry):
        @pl.when((it >= 1) & (it <= KVH))
        def _():
            relay_second(it - 1)

        @pl.when((it >= 2) & (it <= KVH + 1))
        def _():
            relay_third(it - 2)

        @pl.when(it < KVH)
        def _():
            relay_first(it)

        for i, dec in enumerate(steps):
            pl.when(it == i)(dec)

        @pl.when(it >= 3)
        def _():
            relay_last(it - 3)
            attend(it - 3)

        return carry

    lax.fori_loop(0, KVH + 3, turn_body, 0)

    def drain(h, carry):
        relay_sent(h)
        return carry

    lax.fori_loop(0, KVH, drain, 0)
    out_copy(KVH - 2).wait()
    out_copy(KVH - 1).wait()


def step(*operands):
    vmem = pl.BlockSpec(memory_space=pltpu.VMEM)
    hbm = pl.BlockSpec(memory_space=pl.ANY)
    dma = pltpu.SemaphoreType.DMA
    return pl.pallas_call(
        step_kernel,
        out_shape=(
            jax.ShapeDtypeStruct((ROWS, D), BF16),
            jax.ShapeDtypeStruct((REQS, 64), BF16),
        ),
        in_specs=[hbm] * 14,
        out_specs=(hbm, vmem),
        scratch_shapes=[
            pltpu.VMEM((1, 32), jnp.int32),
            pltpu.VMEM((1, 32), jnp.int32),
            pltpu.VMEM((32, 1024), BF16),
            pltpu.VMEM((32, 128), BF16),
            pltpu.VMEM((32, 128), BF16),
            pltpu.VMEM((32, 512), BF16),
            pltpu.VMEM((1, 512), BF16),
            pltpu.VMEM((SEQ, KVH, 2, ROWS, HD), BF16),
            pltpu.VMEM((ROWS, D), BF16),
            pltpu.VMEM((2, ROWS, 1024), BF16),
            pltpu.VMEM((ROWS, 128), BF16),
            pltpu.VMEM((SEQ * ROWS, 128), BF16),
            pltpu.VMEM((ROWS, 128), F32),
            pltpu.VMEM((GROUPED, ROWS, 128), F32),
            pltpu.VMEM((GROUPED, ROWS, 128), F32),
            pltpu.VMEM((GROUPED, ROWS, 128), F32),
            pltpu.VMEM((1024, 512), BF16),
            pltpu.VMEM((512, 2048), BF16),
            pltpu.VMEM((512, 2048), BF16),
            pltpu.VMEM((2048, 512), BF16),
            pltpu.VMEM((32, 128), BF16),
            pltpu.VMEM((8, 32, 128), BF16),
            pltpu.VMEM((8, 2, 32, 128), F32),
            pltpu.VMEM((8, 2, 32, 128), F32),
            pltpu.VMEM((32, 128), BF16),
            pltpu.VMEM((16, 32, 128), BF16),
            pltpu.VMEM((4, 32, 128), F32),
            pltpu.VMEM((8, 32, 128), F32),
            pltpu.VMEM((32, 128), F32),
            pltpu.VMEM((4, 32, 128), F32),
            pltpu.VMEM((16, 72, 128), F32),
            pltpu.VMEM((16, 72, 128), F32),
            pltpu.VMEM((32, 128), BF16),
            pltpu.VMEM((16, 32, 128), BF16),
            pltpu.VMEM((4, 32, 128), F32),
            pltpu.VMEM((8, 32, 128), F32),
            dma((7,)),
            dma((4,)),
            dma((8, 2)),
            dma((8,)),
            dma((2,)),
            dma((8, 7)),
            dma((8, 8)),
        ]
        + [dma((8,))] * 4
        + [dma((16,))] * 2
        + [dma((8,))] * 2
        + [dma((4,))] * 2
        + [dma((16,))] * 4
        + [dma((8,))] * 2,
        compiler_params=pltpu.CompilerParams(collective_id=0, has_side_effects=True, vmem_limit_bytes=58 << 20),
        name="step",
    )(*operands)


def shards(
    lengths, group_of, query_pre, key_pre, value_pre, query_new, key_new, value_new,
    hidden_new, out_weight, norm_gain, gate_weight, up_weight, down_weight,
):
    return step(
        lengths.reshape(1, -1), group_of.reshape(1, -1), query_new, key_new, value_new, hidden_new,
        norm_gain.reshape(1, -1), out_weight, gate_weight, up_weight, down_weight, query_pre, key_pre, value_pre,
    )


def solution(mesh):
    both = P(("grp", "seq"), None)
    return jax.shard_map(
        shards,
        mesh=mesh,
        in_specs=(
            P(), P(), both, both, both, P(None, "seq"), P(None, "seq"), P(None, "seq"), P(None, "grp"),
            P("seq", "grp"), P("grp"), P("grp", "seq"), P("grp", "seq"), P("seq", "grp"),
        ),
        out_specs=(both, P(None, ("grp", "seq"))),
        check_vma=False,
    )
```

```python
import functools
import math

import jax
import jax.numpy as jnp
from jax import lax
from jax.experimental import pallas as pl
from jax.experimental.pallas import tpu as pltpu
from jax.sharding import PartitionSpec as P

HD = 128
SEQ = 8
GRP = 16
ROWS = 256
KVH = 8
LAG = 5
GROUPED = 8
REQS = 32
D = 8192
SCALE = 1.0 / math.sqrt(HD)
LOG2E = math.log2(math.e)
NEGATIVE = -1e30
FAR = -float(2**23)
F32 = jnp.float32
BF16 = jnp.bfloat16
NT = (((1,), (1,)), ((), ()))


def iota(shape, dim):
    return lax.broadcasted_iota(jnp.int32, shape, dim)


def as_column(row, count):
    eye = iota((count, 128), 0) == iota((count, 128), 1)
    return jnp.sum(jnp.where(eye, row, 0), axis=1, keepdims=True)


def request_tables(len_ref, grp_ref):
    lengths = jnp.concatenate([len_ref[...], jnp.zeros((1, 128 - REQS), jnp.int32)], 1)
    groups = jnp.concatenate([grp_ref[...], jnp.full((1, 128 - REQS), -1, jnp.int32)], 1)
    len_col = as_column(lengths, 128)
    grp_col = as_column(groups, 128)
    before = (grp_col == groups) & (iota((128, 128), 0) < iota((128, 128), 1))
    starts = jnp.sum(jnp.where(before, len_col, 0), axis=0, keepdims=True)
    ranks = jnp.sum(jnp.where(before, 1, 0), axis=0, keepdims=True)
    return lengths, groups, starts, ranks


def owner_onehot(tables, group, first, count):
    lengths, groups, starts, _ = tables
    slot = first + iota((count, 128), 0)
    return (groups == group) & (slot >= starts) & (slot < starts + lengths)


def remote(src, dst, send_sem, recv_sem, device):
    return pltpu.make_async_remote_copy(src_ref=src, dst_ref=dst, send_sem=send_sem, recv_sem=recv_sem, device_id=device)


class Exchange:
    def __init__(self, axis, count, me, source, landing, send_sem, recv_sem, spread=lambda i: i):
        self.axis, self.count, self.me, self.spread = axis, count, me, spread
        self.source, self.landing, self.send_sem, self.recv_sem = source, landing, send_sem, recv_sem

    def start(self):
        for i in range(1, self.count):
            peer = (self.me + i) % self.count
            remote(
                self.source(peer),
                self.landing.at[self.me],
                self.send_sem.at[i],
                self.recv_sem.at[self.me],
                {self.axis: self.spread(peer)},
            ).start()

    def wait(self):
        for i in range(1, self.count):
            peer = (self.me + i) % self.count
            copy = remote(
                self.source(peer),
                self.landing.at[peer],
                self.send_sem.at[i],
                self.recv_sem.at[peer],
                {self.axis: self.spread(peer)},
            )
            copy.wait_send()
            copy.wait_recv()


def step_kernel(
    len_hbm, grp_hbm, qn_hbm, kn_hbm, vn_hbm, hid_hbm, gain_hbm, ow_ref, gw_ref, uw_ref, dw_ref, q_ref, k_ref, v_ref,
    out_ref, dec_ref,
    len_ref, grp_ref, qn_ref, kn_ref, vn_ref, hid_ref, gain_ref,
    kvg, qb, ob, qx, kx, live, top, total, accum,
    owb, gwb, uwb, dwb, qmsg, qall, pmsg, part, amsg, aall, pblk, prs, rmsg, rall, gmsg, grs, hmsg, hall, dblk, drs,
    isem, wsem, lsem, qsem, osem, kss, krs, qss, qrs, pss, prsem, ass, ars, oss, ors, rss, rrs, gss, grsem, hss, hrs, dss, drsem,
):
    seq = lax.axis_index("seq")
    group = lax.axis_index("grp")
    y, z = seq // 2, seq % 2
    pair = seq + 1 - 2 * z
    up, down = (seq + 2) % SEQ, (seq + 6) % SEQ

    barrier = pltpu.get_barrier_semaphore()
    for i in range(1, SEQ):
        pl.semaphore_signal(barrier, inc=1, device_id={"seq": (seq + i) % SEQ})
    for i in range(1, GRP):
        pl.semaphore_signal(barrier, inc=1, device_id={"grp": (group + i) % GRP})

    def own_copy(h, which):
        src = (k_ref, v_ref)[which].at[:, pl.ds(pl.multiple_of(h * HD, HD), HD)]
        return pltpu.make_async_copy(src, kvg.at[seq, h, which], lsem.at[h, which])

    def own_start(h, carry):
        own_copy(h, 0).start()
        own_copy(h, 1).start()
        return carry

    small = [
        (len_hbm, len_ref), (grp_hbm, grp_ref), (qn_hbm, qn_ref), (kn_hbm, kn_ref),
        (vn_hbm, vn_ref), (hid_hbm, hid_ref), (gain_hbm, gain_ref),
    ]
    for i, (src, dst) in enumerate(small):
        pltpu.make_async_copy(src, dst, isem.at[i]).start()
    lax.fori_loop(0, KVH, own_start, 0)

    def q_copy(h):
        cols = pl.ds(pl.multiple_of(h * 1024, 1024), 1024)
        return pltpu.make_async_copy(q_ref.at[:, cols], qb.at[:, cols], qsem.at[h])

    def out_copy(h):
        cols = pl.ds(pl.multiple_of(h * 1024, 1024), 1024)
        return pltpu.make_async_copy(ob.at[h % 2], out_ref.at[:, cols], osem.at[h % 2])

    weights = [(ow_ref, owb), (gw_ref, gwb), (uw_ref, uwb), (dw_ref, dwb)]
    for i, (src, dst) in enumerate(weights):
        pltpu.make_async_copy(src, dst, wsem.at[i]).start()

    def weight_wait(i):
        pltpu.make_async_copy(weights[i][0], weights[i][1], wsem.at[i]).wait()

    def q_start(h, carry):
        q_copy(h).start()
        return carry

    lax.fori_loop(0, KVH, q_start, 0)
    for i, (src, dst) in enumerate(small):
        pltpu.make_async_copy(src, dst, isem.at[i]).wait()

    tables = request_tables(len_ref, grp_ref)
    lengths, groups, starts, ranks = tables
    slot32 = iota((REQS, 128), 0) % 4
    pick = (groups == group) & (ranks == slot32)
    pick32 = jnp.where(pick, 1.0, 0.0).astype(BF16)[:, 0:REQS]
    block32 = iota((REQS, HD), 0) // 4
    spread_q = jnp.dot(pick32, qn_ref[...], preferred_element_type=F32)
    mine_q = jnp.zeros((REQS, HD), F32)
    for a in range(GROUPED):
        mine_q = mine_q + jnp.where(block32 == a, spread_q[:, a * HD : (a + 1) * HD], 0.0)
    qmsg[...] = mine_q.astype(BF16)
    qall[seq] = mine_q.astype(BF16)

    lane = iota((ROWS, 128), 1)
    rows_in = owner_onehot(tables, group, seq * ROWS, ROWS)
    qx[...] = jnp.where(((lane < REQS) & jnp.logical_not(rows_in)) | (lane == 127), FAR, 0.0).astype(BF16)
    held = jnp.sum(jnp.where(rows_in, 1.0, 0.0), axis=1, keepdims=True)
    live[...] = jnp.broadcast_to(held, (ROWS, 128))
    for t in range(SEQ):
        cols_in = owner_onehot(tables, group, t * ROWS, ROWS)
        none = jnp.sum(jnp.where(cols_in, 1.0, 0.0), axis=1, keepdims=True) == 0.0
        kx[t * ROWS : (t + 1) * ROWS, :] = jnp.where(cols_in | (none & (lane == 127)), 1.0, 0.0).astype(BF16)

    def own_wait(h, carry):
        own_copy(h, 0).wait()
        own_copy(h, 1).wait()
        return carry

    lax.fori_loop(0, KVH, own_wait, 0)
    pl.semaphore_wait(barrier, SEQ + GRP - 2)

    ex_q = Exchange("seq", SEQ, seq, lambda p: qmsg, qall, qss, qrs)
    ex_p = Exchange("seq", SEQ, seq, lambda p: pmsg.at[p], part, pss, prsem)
    ex_a = Exchange("grp", GRP, group, lambda p: amsg, aall, ass, ars)
    ex_o = Exchange("seq", SEQ, seq, lambda p: pblk.at[p // 2], prs, oss, ors)
    ex_r = Exchange("seq", 4, y, lambda p: rmsg, rall, rss, rrs, lambda p: 2 * p + z)
    ex_g = Exchange("grp", GRP, group, lambda p: gmsg.at[p], grs, gss, grsem)
    ex_h = Exchange("grp", GRP, group, lambda p: hmsg, hall, hss, hrs)
    ex_d = Exchange("seq", SEQ, seq, lambda p: dblk.at[p // 2], drs, dss, drsem)

    def relay(h, slot, shard, dst):
        return remote(kvg.at[shard, h], kvg.at[shard, h], kss.at[h, slot], krs.at[shard, h], {"seq": dst})

    turn = ((y + 1) // 2 + 1) % 2
    cross = 2 * (1 - y % 2) + z
    far = (seq + 4) % SEQ

    def sends(h):
        return [
            (0, seq, pair, y >= 0),
            (1, seq, up, y < 3),
            (2, seq, down, (y == 0) | ((y == 1) & (h % 2 == 1))),
            (3, pair, up, y < 3),
            (4, pair, down, y == 0),
            (5, cross, (seq + 2 + 4 * turn) % SEQ, h % 2 == turn),
            (6, far, pair, y >= 2),
        ]

    def start(h, slots):
        for slot, shard, dst, on in sends(h):
            if slot in slots:

                @pl.when(on)
                def _():
                    relay(h, slot, shard, dst).start()

    def arrived(h, shard):
        relay(h, 0, shard, pair).wait_recv()

    def relay_pair(h):
        start(h, (0,))

    def relay_own(h):
        start(h, (1, 2))

    def relay_other(h):
        start(h, (3, 4))

    def relay_cross(h):
        @pl.when(h % 2 == turn)
        def _():
            arrived(h, cross)

        start(h, (5,))

    def relay_far(h):
        @pl.when(y >= 2)
        def _():
            arrived(h, far)

        start(h, (6,))

    def relay_last(h):
        for t in range(SEQ):
            seen = ((t == cross) & (h % 2 == turn)) | ((t == far) & (y >= 2))

            @pl.when((t // 2 < y) & jnp.logical_not(seen))
            def _():
                arrived(h, t)

    def relay_sent(h):
        for slot, shard, dst, on in sends(h):

            @pl.when(on)
            def _():
                relay(h, slot, shard, dst).wait_send()

    def dec0():
        ex_q.start()

    def dec1():
        ex_q.wait()
        start_c = jnp.sum(jnp.where(pick, starts, 0), axis=1, keepdims=True)
        len_c = jnp.sum(jnp.where(pick, lengths, 0), axis=1, keepdims=True)
        pos = seq * ROWS + iota((REQS, ROWS), 1)
        allowed = (pos >= start_c) & (pos < start_c + len_c)
        for t in range(SEQ):
            s = lax.dot_general(qall[t], kvg[seq, t, 0], NT, preferred_element_type=F32) * SCALE
            s = jnp.where(allowed, s, NEGATIVE)
            m = jnp.max(s, axis=1, keepdims=True)
            p = jnp.where(allowed, jnp.exp(s - m), 0.0)
            l = jnp.sum(p, axis=1, keepdims=True)
            pmsg[t, 0] = jnp.dot(p.astype(BF16), kvg[seq, t, 1], preferred_element_type=F32)
            pmsg[t, 1] = jnp.where(iota((REQS, HD), 1) == 0, m, l)
        part[seq] = pmsg[seq]
        ex_p.start()

    def dec2():
        ex_p.wait()
        key_row = jnp.dot(pick32, kn_ref[...], preferred_element_type=F32)
        value_row = jnp.dot(pick32, vn_ref[...], preferred_element_type=F32)
        own = jnp.sum(qmsg[...].astype(F32) * key_row, axis=1, keepdims=True) * SCALE
        top = own
        for t in range(SEQ):
            top = jnp.maximum(top, part[t, 1][:, 0:1])
        weight = jnp.exp(own - top)
        total = weight
        mixed = weight.astype(BF16).astype(F32) * value_row
        for t in range(SEQ):
            scale = jnp.exp(part[t, 1][:, 0:1] - top)
            total = total + scale * part[t, 1][:, 1:2]
            mixed = mixed + scale * part[t, 0]
        out = (mixed / total).astype(BF16)
        amsg[...] = out
        aall[group] = out
        ex_a.start()

    def dec3():
        ex_a.wait()
        rank_col = as_column(ranks, REQS)
        grp_col = as_column(groups, REQS)
        target = jnp.concatenate([grp_col * 32 + a * 4 + rank_col for a in range(GROUPED)], 0)
        gather = jnp.where(iota((256, 512), 1) == target, 1.0, 0.0).astype(BF16)
        rows = jnp.dot(gather, aall[...].reshape(512, HD), preferred_element_type=F32).astype(BF16)
        att = jnp.concatenate([rows[a * 32 : (a + 1) * 32] for a in range(GROUPED)], 1)
        weight_wait(0)
        proj = jnp.dot(att, owb[...], preferred_element_type=F32)
        for b in range(4):
            pblk[b] = proj[:, b * 128 : (b + 1) * 128]
        prs[seq] = pblk[y]
        ex_o.start()

    def dec4():
        ex_o.wait()
        r = hid_ref[:, pl.ds(pl.multiple_of(y * 128, 128), 128)].astype(F32)
        for t in range(SEQ):
            r = r + prs[t]
        rmsg[...] = r
        rall[y] = r
        ex_r.start()

    def dec5():
        ex_r.wait()
        r = jnp.concatenate([rall[b] for b in range(4)], 1)
        squares = jnp.sum(r * r, axis=1, keepdims=True)
        x = (r * gain_ref[...].astype(F32)).astype(BF16)
        eye = iota((REQS, 128), 0) == iota((REQS, 128), 1)
        row = jnp.sum(jnp.where(eye, squares, 0.0), axis=0, keepdims=True)
        weight_wait(1)
        weight_wait(2)
        gate = jnp.dot(x, gwb[...], preferred_element_type=F32)
        upper = jnp.dot(x, uwb[...], preferred_element_type=F32)
        for t in range(GRP):
            gmsg[t, 0:32] = gate[:, t * 128 : (t + 1) * 128]
            gmsg[t, 32:64] = upper[:, t * 128 : (t + 1) * 128]
            gmsg[t, 64:72] = jnp.broadcast_to(row, (8, 128))
        grs[group] = gmsg[group]
        ex_g.start()

    def dec6():
        ex_g.wait()
        acc = grs[0]
        for t in range(1, GRP):
            acc = acc + grs[t]
        squares = as_column(acc[64:65, :], REQS)
        r = lax.rsqrt(squares / D + 1e-05)
        gate = acc[0:32] * r
        upper = acc[32:64] * r
        out = (gate / (1.0 + jnp.exp(-gate)) * upper).astype(BF16)
        hmsg[...] = out
        hall[group] = out
        ex_h.start()

    def dec7():
        ex_h.wait()
        hidden = jnp.concatenate([hall[t] for t in range(GRP)], 1)
        weight_wait(3)
        out = jnp.dot(hidden, dwb[...], preferred_element_type=F32)
        for b in range(4):
            dblk[b] = out[:, b * 128 : (b + 1) * 128]
        drs[seq] = dblk[y]
        ex_d.start()

    def dec8():
        ex_d.wait()
        out = rmsg[...]
        for t in range(SEQ):
            out = out + drs[t]
        dec_ref[...] = jnp.where(z == 0, out[:, 0:64], out[:, 64:128]).astype(BF16)

    steps = [dec0, dec1, dec2, dec3, dec4, dec5, dec6, dec7, dec8]

    def products(h, j):
        keys = kvg[pl.ds(2 * j, 2), h, 0].reshape(512, HD)
        keys = jnp.concatenate([keys, kx[pl.ds(pl.multiple_of(j * 512, 512), 512), :]], 1)
        scores = []
        for a in range(GROUPED):
            cols = pl.ds(pl.multiple_of((h * GROUPED + a) * HD, HD), HD)
            queries = jnp.concatenate([qb[:, cols], qx[...]], 1)
            scores.append(lax.dot_general(queries, keys, NT, preferred_element_type=F32))
        return scores

    def folded(parts, op):
        return functools.reduce(op, [parts[:, i * 128 : (i + 1) * 128] for i in range(4)])

    def weigh(s, new):
        shift = new * (SCALE * LOG2E)
        return jnp.concatenate(
            [jnp.exp2(s[:, i * 128 : (i + 1) * 128] * (SCALE * LOG2E) - shift) for i in range(4)], 1
        )

    def diagonal(h):
        arrived(h, pair)
        q_copy(h).wait()
        values = kvg[pl.ds(2 * y, 2), h, 1].reshape(512, HD)
        causal = (y * 512 + iota((ROWS, 512), 1)) <= (seq * ROWS + iota((ROWS, 512), 0))
        scores = products(h, y)
        for a in range(GROUPED):
            s = jnp.where(causal, scores[a], NEGATIVE)
            new = jnp.max(folded(s, jnp.maximum), axis=1, keepdims=True)
            new = jnp.broadcast_to(new, (ROWS, 128))
            p = weigh(s, new)
            total[h, a] = folded(p, jnp.add)
            top[h, a] = new
            accum[h, a] = jnp.dot(p.astype(BF16), values, preferred_element_type=F32)

    def block(h, j):
        values = kvg[pl.ds(2 * j, 2), h, 1].reshape(512, HD)
        scores = products(h, j)
        for a in range(GROUPED):
            s = scores[a]
            old = top[h, a]
            new = jnp.maximum(old, jnp.max(folded(s, jnp.maximum), axis=1, keepdims=True))
            decay = jnp.exp2((old - new) * (SCALE * LOG2E))
            p = weigh(s, new)
            total[h, a] = total[h, a] * decay + folded(p, jnp.add)
            top[h, a] = new
            accum[h, a] = accum[h, a] * decay + jnp.dot(p.astype(BF16), values, preferred_element_type=F32)

    def when_head(h, action):
        @pl.when(h < KVH)
        def _():
            action(h)

    def middle(h):
        when_head(h + 1, relay_far)
        when_head(h + 6, relay_pair)
        when_head(h + 3, relay_cross)
        when_head(h + 3, relay_other)
        when_head(h + 5, relay_own)

    def rest(h):
        def each(j, carry):
            @pl.when(j == y // 2)
            def _():
                middle(h)

            block(h, j)
            return carry

        lax.fori_loop(0, y, each, 0)

        @pl.when(y == 0)
        def _():
            middle(h)

        @pl.when(h >= 2)
        def _():
            out_copy(h).wait()

        for a in range(GROUPED):
            t = jnp.sum(total[h, a], axis=1, keepdims=True)
            ok = live[...] > 0.0
            ob[h % 2, :, a * HD : (a + 1) * HD] = jnp.where(ok, accum[h, a] / t, 0.0).astype(BF16)
        out_copy(h).start()

    relay_pair(0)
    relay_own(0)
    dec0()
    relay_pair(1)
    relay_own(1)
    relay_pair(2)
    relay_pair(3)
    opening = {
        0: [(relay_cross, 0), (relay_other, 0), (relay_own, 2), (dec1, None)],
        1: [(relay_far, 0), (relay_pair, 4)],
        2: [(relay_cross, 1), (relay_other, 1), (relay_own, 3)],
        3: [(relay_pair, 5), (dec2, None)],
        4: [(relay_cross, 2), (relay_other, 2), (relay_own, 4)],
    }

    def open_head(i, carry):
        diagonal(i)
        for k, actions in opening.items():

            @pl.when(i == k)
            def _():
                for action, head in actions:
                    action() if head is None else action(head)

        return carry

    def turn_body(i, carry):
        @pl.when(i >= LAG)
        def _():
            relay_last(i - LAG)
            rest(i - LAG)

        @pl.when(i < KVH)
        def _():
            open_head(i, 0)

        for k, dec in enumerate(steps[3:]):
            pl.when(i == LAG + k)(dec)
        return carry

    lax.fori_loop(0, KVH + LAG, turn_body, 0)

    def drain(h, carry):
        relay_sent(h)
        return carry

    lax.fori_loop(0, KVH, drain, 0)
    out_copy(KVH - 2).wait()
    out_copy(KVH - 1).wait()


def step(*operands):
    vmem = pl.BlockSpec(memory_space=pltpu.VMEM)
    hbm = pl.BlockSpec(memory_space=pl.ANY)
    dma = pltpu.SemaphoreType.DMA
    return pl.pallas_call(
        step_kernel,
        out_shape=(
            jax.ShapeDtypeStruct((ROWS, D), BF16),
            jax.ShapeDtypeStruct((REQS, 64), BF16),
        ),
        in_specs=[hbm] * 14,
        out_specs=(hbm, vmem),
        scratch_shapes=[
            pltpu.VMEM((1, 32), jnp.int32),
            pltpu.VMEM((1, 32), jnp.int32),
            pltpu.VMEM((32, 1024), BF16),
            pltpu.VMEM((32, 128), BF16),
            pltpu.VMEM((32, 128), BF16),
            pltpu.VMEM((32, 512), BF16),
            pltpu.VMEM((1, 512), BF16),
            pltpu.VMEM((SEQ, KVH, 2, ROWS, HD), BF16),
            pltpu.VMEM((ROWS, D), BF16),
            pltpu.VMEM((2, ROWS, 1024), BF16),
            pltpu.VMEM((ROWS, 128), BF16),
            pltpu.VMEM((SEQ * ROWS, 128), BF16),
            pltpu.VMEM((ROWS, 128), F32),
            pltpu.VMEM((KVH, GROUPED, ROWS, 128), F32),
            pltpu.VMEM((KVH, GROUPED, ROWS, 128), F32),
            pltpu.VMEM((KVH, GROUPED, ROWS, 128), F32),
            pltpu.VMEM((1024, 512), BF16),
            pltpu.VMEM((512, 2048), BF16),
            pltpu.VMEM((512, 2048), BF16),
            pltpu.VMEM((2048, 512), BF16),
            pltpu.VMEM((32, 128), BF16),
            pltpu.VMEM((8, 32, 128), BF16),
            pltpu.VMEM((8, 2, 32, 128), F32),
            pltpu.VMEM((8, 2, 32, 128), F32),
            pltpu.VMEM((32, 128), BF16),
            pltpu.VMEM((16, 32, 128), BF16),
            pltpu.VMEM((4, 32, 128), F32),
            pltpu.VMEM((8, 32, 128), F32),
            pltpu.VMEM((32, 128), F32),
            pltpu.VMEM((4, 32, 128), F32),
            pltpu.VMEM((16, 72, 128), F32),
            pltpu.VMEM((16, 72, 128), F32),
            pltpu.VMEM((32, 128), BF16),
            pltpu.VMEM((16, 32, 128), BF16),
            pltpu.VMEM((4, 32, 128), F32),
            pltpu.VMEM((8, 32, 128), F32),
            dma((7,)),
            dma((4,)),
            dma((8, 2)),
            dma((8,)),
            dma((2,)),
            dma((8, 7)),
            dma((8, 8)),
        ]
        + [dma((8,))] * 4
        + [dma((16,))] * 2
        + [dma((8,))] * 2
        + [dma((4,))] * 2
        + [dma((16,))] * 4
        + [dma((8,))] * 2,
        compiler_params=pltpu.CompilerParams(collective_id=0, has_side_effects=True, vmem_limit_bytes=58 << 20),
        name="step",
    )(*operands)


def shards(
    lengths, group_of, query_pre, key_pre, value_pre, query_new, key_new, value_new,
    hidden_new, out_weight, norm_gain, gate_weight, up_weight, down_weight,
):
    return step(
        lengths.reshape(1, -1), group_of.reshape(1, -1), query_new, key_new, value_new, hidden_new,
        norm_gain.reshape(1, -1), out_weight, gate_weight, up_weight, down_weight, query_pre, key_pre, value_pre,
    )


def solution(mesh):
    both = P(("grp", "seq"), None)
    return jax.shard_map(
        shards,
        mesh=mesh,
        in_specs=(
            P(), P(), both, both, both, P(None, "seq"), P(None, "seq"), P(None, "seq"), P(None, "grp"),
            P("seq", "grp"), P("grp"), P("grp", "seq"), P("grp", "seq"), P("seq", "grp"),
        ),
        out_specs=(both, P(None, ("grp", "seq"))),
        check_vma=False,
    )
```

```python
import functools
import math

import jax
import jax.numpy as jnp
from jax import lax
from jax.experimental import pallas as pl
from jax.experimental.pallas import tpu as pltpu
from jax.sharding import PartitionSpec as P

HD = 128
SEQ = 8
GRP = 16
ROWS = 256
KVH = 8
GROUPED = 8
REQS = 32
D = 8192
SCALE = 1.0 / math.sqrt(HD)
LOG2E = math.log2(math.e)
NEGATIVE = -1e30
FAR = -float(2**23)
F32 = jnp.float32
BF16 = jnp.bfloat16
NT = (((1,), (1,)), ((), ()))


def iota(shape, dim):
    return lax.broadcasted_iota(jnp.int32, shape, dim)


def as_column(row, count):
    eye = iota((count, 128), 0) == iota((count, 128), 1)
    return jnp.sum(jnp.where(eye, row, 0), axis=1, keepdims=True)


def request_tables(len_ref, grp_ref):
    lengths = jnp.concatenate([len_ref[...].reshape(1, -1), jnp.zeros((1, 128 - REQS), jnp.int32)], 1)
    groups = jnp.concatenate([grp_ref[...].reshape(1, -1), jnp.full((1, 128 - REQS), -1, jnp.int32)], 1)
    len_col = as_column(lengths, 128)
    grp_col = as_column(groups, 128)
    before = (grp_col == groups) & (iota((128, 128), 0) < iota((128, 128), 1))
    starts = jnp.sum(jnp.where(before, len_col, 0), axis=0, keepdims=True)
    ranks = jnp.sum(jnp.where(before, 1, 0), axis=0, keepdims=True)
    return lengths, groups, starts, ranks


def owner_onehot(tables, group, first, count):
    lengths, groups, starts, _ = tables
    slot = first + iota((count, 128), 0)
    return (groups == group) & (slot >= starts) & (slot < starts + lengths)


def remote(src, dst, send_sem, recv_sem, device):
    return pltpu.make_async_remote_copy(src_ref=src, dst_ref=dst, send_sem=send_sem, recv_sem=recv_sem, device_id=device)


class Exchange:
    def __init__(self, axis, count, me, source, landing, send_sem, recv_sem, spread=lambda i: i):
        self.axis, self.count, self.me, self.spread = axis, count, me, spread
        self.source, self.landing, self.send_sem, self.recv_sem = source, landing, send_sem, recv_sem

    def start(self):
        for i in range(1, self.count):
            peer = (self.me + i) % self.count
            remote(
                self.source(peer),
                self.landing.at[self.me],
                self.send_sem.at[i],
                self.recv_sem.at[self.me],
                {self.axis: self.spread(peer)},
            ).start()

    def wait(self):
        for i in range(1, self.count):
            peer = (self.me + i) % self.count
            copy = remote(
                self.source(peer),
                self.landing.at[peer],
                self.send_sem.at[i],
                self.recv_sem.at[peer],
                {self.axis: self.spread(peer)},
            )
            copy.wait_send()
            copy.wait_recv()


def step_kernel(
    len_hbm, grp_hbm, qn_hbm, kn_hbm, vn_hbm, hid_hbm, gain_hbm, ow_ref, gw_ref, uw_ref, dw_ref, q_ref, k_ref, v_ref,
    out_ref, dec_ref,
    len_ref, grp_ref, qn_ref, kn_ref, vn_ref, hid_ref, gain_ref,
    kvg, qb, ob, qx, kx, live, top, total, accum,
    owb, gwb, uwb, dwb, qmsg, qall, pmsg, part, amsg, aall, pblk, prs, rmsg, rall, gmsg, grs, hmsg, hall, dblk, drs,
    isem, wsem, lsem, qsem, osem, kss, krs, qss, qrs, pss, prsem, ass, ars, oss, ors, rss, rrs, gss, grsem, hss, hrs, dss, drsem,
):
    seq = lax.axis_index("seq")
    group = lax.axis_index("grp")
    y, z = seq // 2, seq % 2
    pair = seq + 1 - 2 * z
    up, down = (seq + 2) % SEQ, (seq + 6) % SEQ

    barrier = pltpu.get_barrier_semaphore()
    for i in range(1, SEQ):
        pl.semaphore_signal(barrier, inc=1, device_id={"seq": (seq + i) % SEQ})
    for i in range(1, GRP):
        pl.semaphore_signal(barrier, inc=1, device_id={"grp": (group + i) % GRP})

    def own_copy(h, which):
        src = (k_ref, v_ref)[which].at[:, pl.ds(pl.multiple_of(h * HD, HD), HD)]
        return pltpu.make_async_copy(src, kvg.at[seq, h, which], lsem.at[h, which])

    def own_start(h, carry):
        own_copy(h, 0).start()
        own_copy(h, 1).start()
        return carry

    small = [
        (len_hbm, len_ref), (grp_hbm, grp_ref), (qn_hbm, qn_ref), (kn_hbm, kn_ref),
        (vn_hbm, vn_ref), (hid_hbm, hid_ref), (gain_hbm, gain_ref),
    ]
    for i, (src, dst) in enumerate(small):
        pltpu.make_async_copy(src, dst, isem.at[i]).start()
    lax.fori_loop(0, KVH, own_start, 0)

    def q_copy(h):
        cols = pl.ds(pl.multiple_of(h * 1024, 1024), 1024)
        return pltpu.make_async_copy(q_ref.at[:, cols], qb.at[:, cols], qsem.at[h])

    def out_copy(h):
        cols = pl.ds(pl.multiple_of(h * 1024, 1024), 1024)
        return pltpu.make_async_copy(ob.at[h % 2], out_ref.at[:, cols], osem.at[h % 2])

    weights = [(ow_ref, owb), (gw_ref, gwb), (uw_ref, uwb), (dw_ref, dwb)]
    for i, (src, dst) in enumerate(weights):
        pltpu.make_async_copy(src, dst, wsem.at[i]).start()

    def weight_wait(i):
        pltpu.make_async_copy(weights[i][0], weights[i][1], wsem.at[i]).wait()

    def q_start(h, carry):
        q_copy(h).start()
        return carry

    lax.fori_loop(0, KVH, q_start, 0)
    for i, (src, dst) in enumerate(small):
        pltpu.make_async_copy(src, dst, isem.at[i]).wait()

    tables = request_tables(len_ref, grp_ref)
    lengths, groups, starts, ranks = tables
    slot32 = iota((REQS, 128), 0) % 4
    pick = (groups == group) & (ranks == slot32)
    pick32 = jnp.where(pick, 1.0, 0.0).astype(BF16)[:, 0:REQS]
    block32 = iota((REQS, HD), 0) // 4
    spread_q = jnp.dot(pick32, qn_ref[...], preferred_element_type=F32)
    mine_q = jnp.zeros((REQS, HD), F32)
    for a in range(GROUPED):
        mine_q = mine_q + jnp.where(block32 == a, spread_q[:, a * HD : (a + 1) * HD], 0.0)
    qmsg[...] = mine_q.astype(BF16)
    qall[seq] = mine_q.astype(BF16)

    lane = iota((ROWS, 128), 1)
    rows_in = owner_onehot(tables, group, seq * ROWS, ROWS)
    qx[...] = jnp.where(((lane < REQS) & jnp.logical_not(rows_in)) | (lane == 127), FAR, 0.0).astype(BF16)
    held = jnp.sum(jnp.where(rows_in, 1.0, 0.0), axis=1, keepdims=True)
    live[...] = jnp.broadcast_to(held, (ROWS, 128))
    for t in range(SEQ):
        cols_in = owner_onehot(tables, group, t * ROWS, ROWS)
        none = jnp.sum(jnp.where(cols_in, 1.0, 0.0), axis=1, keepdims=True) == 0.0
        kx[t * ROWS : (t + 1) * ROWS, :] = jnp.where(cols_in | (none & (lane == 127)), 1.0, 0.0).astype(BF16)

    def own_wait(h, carry):
        own_copy(h, 0).wait()
        own_copy(h, 1).wait()
        return carry

    lax.fori_loop(0, KVH, own_wait, 0)
    pl.semaphore_wait(barrier, SEQ + GRP - 2)

    ex_q = Exchange("seq", SEQ, seq, lambda p: qmsg, qall, qss, qrs)
    ex_p = Exchange("seq", SEQ, seq, lambda p: pmsg.at[p], part, pss, prsem)
    ex_a = Exchange("grp", GRP, group, lambda p: amsg, aall, ass, ars)
    ex_o = Exchange("seq", SEQ, seq, lambda p: pblk.at[p // 2], prs, oss, ors)
    ex_r = Exchange("seq", 4, y, lambda p: rmsg, rall, rss, rrs, lambda p: 2 * p + z)
    ex_g = Exchange("grp", GRP, group, lambda p: gmsg.at[p], grs, gss, grsem)
    ex_h = Exchange("grp", GRP, group, lambda p: hmsg, hall, hss, hrs)
    ex_d = Exchange("seq", SEQ, seq, lambda p: dblk.at[p // 2], drs, dss, drsem)

    def relay(h, slot, shard, dst):
        return remote(kvg.at[shard, h], kvg.at[shard, h], kss.at[h, slot], krs.at[shard, h], {"seq": dst})

    turn = ((y + 1) // 2 + 1) % 2
    cross = 2 * (1 - y % 2) + z
    far = (seq + 4) % SEQ

    def sends(h):
        return [
            (0, seq, pair, y >= 0),
            (1, seq, up, y < 3),
            (2, seq, down, (y == 0) | ((y == 1) & (h % 2 == 1))),
            (3, pair, up, y < 3),
            (4, pair, down, y == 0),
            (5, cross, (seq + 2 + 4 * turn) % SEQ, h % 2 == turn),
            (6, far, pair, y >= 2),
        ]

    def start(h, slots):
        for slot, shard, dst, on in sends(h):
            if slot in slots:

                @pl.when(on)
                def _():
                    relay(h, slot, shard, dst).start()

    def arrived(h, shard):
        relay(h, 0, shard, pair).wait_recv()

    def relay_pair(h):
        start(h, (0,))

    def relay_own(h):
        start(h, (1, 2))

    def relay_other(h):
        arrived(h, pair)
        start(h, (3, 4))

    def relay_cross(h):
        @pl.when(h % 2 == turn)
        def _():
            arrived(h, cross)

        start(h, (5,))

    def relay_far(h):
        @pl.when(y >= 2)
        def _():
            arrived(h, far)

        start(h, (6,))

    def relay_last(h):
        for t in range(SEQ):
            seen = ((t == cross) & (h % 2 == turn)) | ((t == far) & (y >= 2))

            @pl.when((t // 2 < y) & jnp.logical_not(seen))
            def _():
                arrived(h, t)

    def relay_sent(h):
        for slot, shard, dst, on in sends(h):

            @pl.when(on)
            def _():
                relay(h, slot, shard, dst).wait_send()

    def dec0():
        ex_q.start()

    def dec1():
        ex_q.wait()
        start_c = jnp.sum(jnp.where(pick, starts, 0), axis=1, keepdims=True)
        len_c = jnp.sum(jnp.where(pick, lengths, 0), axis=1, keepdims=True)
        pos = seq * ROWS + iota((REQS, ROWS), 1)
        allowed = (pos >= start_c) & (pos < start_c + len_c)
        for t in range(SEQ):
            s = lax.dot_general(qall[t], kvg[seq, t, 0], NT, preferred_element_type=F32) * SCALE
            s = jnp.where(allowed, s, NEGATIVE)
            m = jnp.max(s, axis=1, keepdims=True)
            p = jnp.where(allowed, jnp.exp(s - m), 0.0)
            l = jnp.sum(p, axis=1, keepdims=True)
            pmsg[t, 0] = jnp.dot(p.astype(BF16), kvg[seq, t, 1], preferred_element_type=F32)
            pmsg[t, 1] = jnp.where(iota((REQS, HD), 1) == 0, m, l)
        part[seq] = pmsg[seq]
        ex_p.start()

    def dec2():
        ex_p.wait()
        key_row = jnp.dot(pick32, kn_ref[...], preferred_element_type=F32)
        value_row = jnp.dot(pick32, vn_ref[...], preferred_element_type=F32)
        own = jnp.sum(qmsg[...].astype(F32) * key_row, axis=1, keepdims=True) * SCALE
        top = own
        for t in range(SEQ):
            top = jnp.maximum(top, part[t, 1][:, 0:1])
        weight = jnp.exp(own - top)
        total = weight
        mixed = weight.astype(BF16).astype(F32) * value_row
        for t in range(SEQ):
            scale = jnp.exp(part[t, 1][:, 0:1] - top)
            total = total + scale * part[t, 1][:, 1:2]
            mixed = mixed + scale * part[t, 0]
        out = (mixed / total).astype(BF16)
        amsg[...] = out
        aall[group] = out
        ex_a.start()

    def dec3():
        ex_a.wait()
        rank_col = as_column(ranks, REQS)
        grp_col = as_column(groups, REQS)
        target = jnp.concatenate([grp_col * 32 + a * 4 + rank_col for a in range(GROUPED)], 0)
        gather = jnp.where(iota((256, 512), 1) == target, 1.0, 0.0).astype(BF16)
        rows = jnp.dot(gather, aall[...].reshape(512, HD), preferred_element_type=F32).astype(BF16)
        att = jnp.concatenate([rows[a * 32 : (a + 1) * 32] for a in range(GROUPED)], 1)
        weight_wait(0)
        proj = jnp.dot(att, owb[...], preferred_element_type=F32)
        for b in range(4):
            pblk[b] = proj[:, b * 128 : (b + 1) * 128]
        prs[seq] = pblk[y]
        ex_o.start()

    def dec4():
        ex_o.wait()
        r = hid_ref[:, pl.ds(pl.multiple_of(y * 128, 128), 128)].astype(F32)
        for t in range(SEQ):
            r = r + prs[t]
        rmsg[...] = r
        rall[y] = r
        ex_r.start()

    def dec5():
        ex_r.wait()
        r = jnp.concatenate([rall[b] for b in range(4)], 1)
        squares = jnp.sum(r * r, axis=1, keepdims=True)
        x = (r * gain_ref[...].astype(F32).reshape(1, -1)).astype(BF16)
        eye = iota((REQS, 128), 0) == iota((REQS, 128), 1)
        row = jnp.sum(jnp.where(eye, squares, 0.0), axis=0, keepdims=True)
        weight_wait(1)
        weight_wait(2)
        gate = jnp.dot(x, gwb[...], preferred_element_type=F32)
        upper = jnp.dot(x, uwb[...], preferred_element_type=F32)
        for t in range(GRP):
            gmsg[t, 0:32] = gate[:, t * 128 : (t + 1) * 128]
            gmsg[t, 32:64] = upper[:, t * 128 : (t + 1) * 128]
            gmsg[t, 64:72] = jnp.broadcast_to(row, (8, 128))
        grs[group] = gmsg[group]
        ex_g.start()

    def dec6():
        ex_g.wait()
        acc = grs[0]
        for t in range(1, GRP):
            acc = acc + grs[t]
        squares = as_column(acc[64:65, :], REQS)
        r = lax.rsqrt(squares / D + 1e-05)
        gate = acc[0:32] * r
        upper = acc[32:64] * r
        out = (gate / (1.0 + jnp.exp(-gate)) * upper).astype(BF16)
        hmsg[...] = out
        hall[group] = out
        ex_h.start()

    def dec7():
        ex_h.wait()
        hidden = jnp.concatenate([hall[t] for t in range(GRP)], 1)
        weight_wait(3)
        out = jnp.dot(hidden, dwb[...], preferred_element_type=F32)
        for b in range(4):
            dblk[b] = out[:, b * 128 : (b + 1) * 128]
        drs[seq] = dblk[y]
        ex_d.start()

    def dec8():
        ex_d.wait()
        out = rmsg[...]
        for t in range(SEQ):
            out = out + drs[t]
        dec_ref[...] = jnp.where(z == 0, out[:, 0:64], out[:, 64:128]).astype(BF16)

    steps = [dec0, dec1, dec2, dec3, dec4, dec5, dec6, dec7, dec8]

    def products(h, keys, first):
        count = keys.shape[0]
        keys = jnp.concatenate([keys, kx[pl.ds(pl.multiple_of(first * ROWS, ROWS), count), :]], 1)
        scores = []
        for a in range(GROUPED):
            cols = pl.ds(pl.multiple_of((h * GROUPED + a) * HD, HD), HD)
            queries = jnp.concatenate([qb[:, cols], qx[...]], 1)
            scores.append(lax.dot_general(queries, keys, NT, preferred_element_type=F32))
        return scores

    def folded(parts, op):
        return functools.reduce(op, [parts[:, i : i + 128] for i in range(0, parts.shape[1], 128)])

    def weigh(s, new):
        shift = new * (SCALE * LOG2E)
        return jnp.concatenate(
            [jnp.exp2(s[:, i : i + 128] * (SCALE * LOG2E) - shift) for i in range(0, s.shape[1], 128)], 1
        )

    def diagonal(h):
        q_copy(h).wait()
        values = kvg[seq, h, 1]
        causal = iota((ROWS, ROWS), 1) <= iota((ROWS, ROWS), 0)
        scores = products(h, kvg[seq, h, 0], seq)
        for a in range(GROUPED):
            s = jnp.where(causal, scores[a], NEGATIVE)
            new = jnp.max(folded(s, jnp.maximum), axis=1, keepdims=True)
            new = jnp.broadcast_to(new, (ROWS, 128))
            p = weigh(s, new)
            total[h, a] = folded(p, jnp.add)
            top[h, a] = new
            accum[h, a] = jnp.dot(p.astype(BF16), values, preferred_element_type=F32)

    def block(h, keys, values, first):
        scores = products(h, keys, first)
        for a in range(GROUPED):
            s = scores[a]
            old = top[h, a]
            new = jnp.maximum(old, jnp.max(folded(s, jnp.maximum), axis=1, keepdims=True))
            decay = jnp.exp2((old - new) * (SCALE * LOG2E))
            p = weigh(s, new)
            total[h, a] = total[h, a] * decay + folded(p, jnp.add)
            top[h, a] = new
            accum[h, a] = accum[h, a] * decay + jnp.dot(p.astype(BF16), values, preferred_element_type=F32)

    def when_head(h, action):
        @pl.when(h < KVH)
        def _():
            action(h)

    def middle(h):
        when_head(h + 1, relay_far)
        when_head(h + 2, relay_cross)
        when_head(h + 2, relay_other)
        when_head(h + 4, relay_own)
        when_head(h + 5, relay_pair)

    def rest(h):
        def each(j, carry):
            @pl.when(j == y // 2)
            def _():
                middle(h)

            keys = kvg[pl.ds(2 * j, 2), h, 0].reshape(512, HD)
            values = kvg[pl.ds(2 * j, 2), h, 1].reshape(512, HD)
            block(h, keys, values, 2 * j)
            return carry

        @pl.when(z == 1)
        def _():
            block(h, kvg[pair, h, 0], kvg[pair, h, 1], pair)

        lax.fori_loop(0, y, each, 0)

        @pl.when(y == 0)
        def _():
            middle(h)

        @pl.when(h >= 2)
        def _():
            out_copy(h).wait()

        for a in range(GROUPED):
            t = jnp.sum(total[h, a], axis=1, keepdims=True)
            ok = live[...] > 0.0
            ob[h % 2, :, a * HD : (a + 1) * HD] = jnp.where(ok, accum[h, a] / t, 0.0).astype(BF16)
        out_copy(h).start()

    relay_pair(0)
    relay_own(0)
    dec0()
    relay_pair(1)
    relay_own(1)
    opening = {
        2: [(relay_cross, 0), (relay_other, 0), (relay_own, 2), (relay_pair, 2)],
        3: [(dec1, None)],
        5: [(relay_far, 0), (relay_pair, 3)],
        6: [(relay_cross, 1), (relay_other, 1), (relay_own, 3), (relay_pair, 4)],
        7: [(dec2, None)],
    }

    def open_head(i, carry):
        diagonal(i)
        for k, actions in opening.items():

            @pl.when(i == k)
            def _():
                for action, head in actions:
                    action() if head is None else action(head)

        return carry

    lax.fori_loop(0, KVH, open_head, 0)

    def close_head(h, carry):
        relay_last(h)
        rest(h)
        for k, dec in enumerate(steps[3:]):
            pl.when(h == k)(dec)
        return carry

    lax.fori_loop(0, KVH, close_head, 0)

    def drain(h, carry):
        relay_sent(h)
        return carry

    lax.fori_loop(0, KVH, drain, 0)
    out_copy(KVH - 2).wait()
    out_copy(KVH - 1).wait()


def step(*operands):
    vmem = pl.BlockSpec(memory_space=pltpu.VMEM)
    hbm = pl.BlockSpec(memory_space=pl.ANY)
    dma = pltpu.SemaphoreType.DMA
    return pl.pallas_call(
        step_kernel,
        out_shape=(
            jax.ShapeDtypeStruct((ROWS, D), BF16),
            jax.ShapeDtypeStruct((REQS, 64), BF16),
        ),
        in_specs=[hbm] * 14,
        out_specs=(hbm, vmem),
        scratch_shapes=[
            pltpu.VMEM((32,), jnp.int32),
            pltpu.VMEM((32,), jnp.int32),
            pltpu.VMEM((32, 1024), BF16),
            pltpu.VMEM((32, 128), BF16),
            pltpu.VMEM((32, 128), BF16),
            pltpu.VMEM((32, 512), BF16),
            pltpu.VMEM((512,), BF16),
            pltpu.VMEM((SEQ, KVH, 2, ROWS, HD), BF16),
            pltpu.VMEM((ROWS, D), BF16),
            pltpu.VMEM((2, ROWS, 1024), BF16),
            pltpu.VMEM((ROWS, 128), BF16),
            pltpu.VMEM((SEQ * ROWS, 128), BF16),
            pltpu.VMEM((ROWS, 128), F32),
            pltpu.VMEM((KVH, GROUPED, ROWS, 128), F32),
            pltpu.VMEM((KVH, GROUPED, ROWS, 128), F32),
            pltpu.VMEM((KVH, GROUPED, ROWS, 128), F32),
            pltpu.VMEM((1024, 512), BF16),
            pltpu.VMEM((512, 2048), BF16),
            pltpu.VMEM((512, 2048), BF16),
            pltpu.VMEM((2048, 512), BF16),
            pltpu.VMEM((32, 128), BF16),
            pltpu.VMEM((8, 32, 128), BF16),
            pltpu.VMEM((8, 2, 32, 128), F32),
            pltpu.VMEM((8, 2, 32, 128), F32),
            pltpu.VMEM((32, 128), BF16),
            pltpu.VMEM((16, 32, 128), BF16),
            pltpu.VMEM((4, 32, 128), F32),
            pltpu.VMEM((8, 32, 128), F32),
            pltpu.VMEM((32, 128), F32),
            pltpu.VMEM((4, 32, 128), F32),
            pltpu.VMEM((16, 72, 128), F32),
            pltpu.VMEM((16, 72, 128), F32),
            pltpu.VMEM((32, 128), BF16),
            pltpu.VMEM((16, 32, 128), BF16),
            pltpu.VMEM((4, 32, 128), F32),
            pltpu.VMEM((8, 32, 128), F32),
            dma((7,)),
            dma((4,)),
            dma((8, 2)),
            dma((8,)),
            dma((2,)),
            dma((8, 7)),
            dma((8, 8)),
        ]
        + [dma((8,))] * 4
        + [dma((16,))] * 2
        + [dma((8,))] * 2
        + [dma((4,))] * 2
        + [dma((16,))] * 4
        + [dma((8,))] * 2,
        compiler_params=pltpu.CompilerParams(collective_id=0, has_side_effects=True, vmem_limit_bytes=58 << 20),
        name="step",
    )(*operands)


def shards(
    lengths, group_of, query_pre, key_pre, value_pre, query_new, key_new, value_new,
    hidden_new, out_weight, norm_gain, gate_weight, up_weight, down_weight,
):
    return step(
        lengths, group_of, query_new, key_new, value_new, hidden_new,
        norm_gain, out_weight, gate_weight, up_weight, down_weight, query_pre, key_pre, value_pre,
    )


def solution(mesh):
    both = P(("grp", "seq"), None)
    return jax.shard_map(
        shards,
        mesh=mesh,
        in_specs=(
            P(), P(), both, both, both, P(None, "seq"), P(None, "seq"), P(None, "seq"), P(None, "grp"),
            P("seq", "grp"), P("grp"), P("grp", "seq"), P("grp", "seq"), P("seq", "grp"),
        ),
        out_specs=(both, P(None, ("grp", "seq"))),
        check_vma=False,
    )
```

```python
import functools
import math

import jax
import jax.numpy as jnp
from jax import lax
from jax.experimental import pallas as pl
from jax.experimental.pallas import tpu as pltpu
from jax.sharding import PartitionSpec as P

HD = 128
SEQ = 8
GRP = 16
ROWS = 256
KVH = 8
GROUPED = 8
REQS = 32
D = 8192
SCALE = 1.0 / math.sqrt(HD)
LOG2E = math.log2(math.e)
NEGATIVE = -1e30
FAR = -float(2**23)
F32 = jnp.float32
BF16 = jnp.bfloat16
NT = (((1,), (1,)), ((), ()))


def iota(shape, dim):
    return lax.broadcasted_iota(jnp.int32, shape, dim)


def as_column(row, count):
    eye = iota((count, 128), 0) == iota((count, 128), 1)
    return jnp.sum(jnp.where(eye, row, 0), axis=1, keepdims=True)


def request_tables(len_ref, grp_ref):
    lengths = jnp.concatenate([len_ref[...].reshape(1, -1), jnp.zeros((1, 128 - REQS), jnp.int32)], 1)
    groups = jnp.concatenate([grp_ref[...].reshape(1, -1), jnp.full((1, 128 - REQS), -1, jnp.int32)], 1)
    len_col = as_column(lengths, 128)
    grp_col = as_column(groups, 128)
    before = (grp_col == groups) & (iota((128, 128), 0) < iota((128, 128), 1))
    starts = jnp.sum(jnp.where(before, len_col, 0), axis=0, keepdims=True)
    ranks = jnp.sum(jnp.where(before, 1, 0), axis=0, keepdims=True)
    return lengths, groups, starts, ranks


def owner_onehot(tables, group, first, count):
    lengths, groups, starts, _ = tables
    slot = first + iota((count, 128), 0)
    return (groups == group) & (slot >= starts) & (slot < starts + lengths)


def remote(src, dst, send_sem, recv_sem, device):
    return pltpu.make_async_remote_copy(src_ref=src, dst_ref=dst, send_sem=send_sem, recv_sem=recv_sem, device_id=device)


class Exchange:
    def __init__(self, axis, count, me, source, landing, send_sem, recv_sem, spread=lambda i: i):
        self.axis, self.count, self.me, self.spread = axis, count, me, spread
        self.source, self.landing, self.send_sem, self.recv_sem = source, landing, send_sem, recv_sem

    def start(self):
        for i in range(1, self.count):
            peer = (self.me + i) % self.count
            remote(
                self.source(peer),
                self.landing.at[self.me],
                self.send_sem.at[i],
                self.recv_sem.at[self.me],
                {self.axis: self.spread(peer)},
            ).start()

    def wait(self):
        for i in range(1, self.count):
            peer = (self.me + i) % self.count
            copy = remote(
                self.source(peer),
                self.landing.at[peer],
                self.send_sem.at[i],
                self.recv_sem.at[peer],
                {self.axis: self.spread(peer)},
            )
            copy.wait_send()
            copy.wait_recv()


def step_kernel(
    len_hbm, grp_hbm, qn_hbm, kn_hbm, vn_hbm, hid_hbm, gain_hbm, ow_ref, gw_ref, uw_ref, dw_ref, q_ref, k_ref, v_ref,
    out_ref, dec_ref,
    len_ref, grp_ref, qn_ref, kn_ref, vn_ref, hid_ref, gain_ref,
    kvg, qb, ob, qx, kx, live, top, total, accum,
    owb, gwb, uwb, dwb, qmsg, qall, pmsg, part, amsg, aall, pblk, prs, rmsg, rall, gmsg, grs, hmsg, hall, dblk, drs,
    isem, wsem, lsem, qsem, osem, kss, krs, qss, qrs, pss, prsem, ass, ars, oss, ors, rss, rrs, gss, grsem, hss, hrs, dss, drsem,
):
    seq = lax.axis_index("seq")
    group = lax.axis_index("grp")
    y, z = seq // 2, seq % 2
    pair = seq + 1 - 2 * z
    up, down = (seq + 2) % SEQ, (seq + 6) % SEQ

    barrier = pltpu.get_barrier_semaphore()
    for i in range(1, SEQ):
        pl.semaphore_signal(barrier, inc=1, device_id={"seq": (seq + i) % SEQ})
    for i in range(1, GRP):
        pl.semaphore_signal(barrier, inc=1, device_id={"grp": (group + i) % GRP})

    def own_copy(h, which):
        src = (k_ref, v_ref)[which].at[:, pl.ds(pl.multiple_of(h * HD, HD), HD)]
        return pltpu.make_async_copy(src, kvg.at[seq, h, which], lsem.at[h, which])

    def own_start(h, carry):
        own_copy(h, 0).start()
        own_copy(h, 1).start()
        return carry

    small = [
        (len_hbm, len_ref), (grp_hbm, grp_ref), (qn_hbm, qn_ref), (kn_hbm, kn_ref),
        (vn_hbm, vn_ref), (hid_hbm, hid_ref), (gain_hbm, gain_ref),
    ]
    for i, (src, dst) in enumerate(small):
        pltpu.make_async_copy(src, dst, isem.at[i]).start()
    lax.fori_loop(0, KVH, own_start, 0)

    def q_copy(h):
        cols = pl.ds(pl.multiple_of(h * 1024, 1024), 1024)
        return pltpu.make_async_copy(q_ref.at[:, cols], qb.at[:, cols], qsem.at[h])

    def out_copy(h):
        cols = pl.ds(pl.multiple_of(h * 1024, 1024), 1024)
        return pltpu.make_async_copy(ob.at[h % 2], out_ref.at[:, cols], osem.at[h % 2])

    weights = [(ow_ref, owb), (gw_ref, gwb), (uw_ref, uwb), (dw_ref, dwb)]
    for i, (src, dst) in enumerate(weights):
        pltpu.make_async_copy(src, dst, wsem.at[i]).start()

    def weight_wait(i):
        pltpu.make_async_copy(weights[i][0], weights[i][1], wsem.at[i]).wait()

    def q_start(h, carry):
        q_copy(h).start()
        return carry

    lax.fori_loop(0, KVH, q_start, 0)
    for i, (src, dst) in enumerate(small):
        pltpu.make_async_copy(src, dst, isem.at[i]).wait()

    tables = request_tables(len_ref, grp_ref)
    lengths, groups, starts, ranks = tables
    slot32 = iota((REQS, 128), 0) % 4
    pick = (groups == group) & (ranks == slot32)
    pick32 = jnp.where(pick, 1.0, 0.0).astype(BF16)[:, 0:REQS]
    block32 = iota((REQS, HD), 0) // 4
    spread_q = jnp.dot(pick32, qn_ref[...], preferred_element_type=F32)
    mine_q = jnp.zeros((REQS, HD), F32)
    for a in range(GROUPED):
        mine_q = mine_q + jnp.where(block32 == a, spread_q[:, a * HD : (a + 1) * HD], 0.0)
    qmsg[...] = mine_q.astype(BF16)
    qall[seq] = mine_q.astype(BF16)

    lane = iota((ROWS, 128), 1)
    rows_in = owner_onehot(tables, group, seq * ROWS, ROWS)
    qx[...] = jnp.where(((lane < REQS) & jnp.logical_not(rows_in)) | (lane == 127), FAR, 0.0).astype(BF16)
    held = jnp.sum(jnp.where(rows_in, 1.0, 0.0), axis=1, keepdims=True)
    live[...] = jnp.broadcast_to(held, (ROWS, 128))
    for t in range(SEQ):
        cols_in = owner_onehot(tables, group, t * ROWS, ROWS)
        none = jnp.sum(jnp.where(cols_in, 1.0, 0.0), axis=1, keepdims=True) == 0.0
        kx[t * ROWS : (t + 1) * ROWS, :] = jnp.where(cols_in | (none & (lane == 127)), 1.0, 0.0).astype(BF16)

    def own_wait(h, carry):
        own_copy(h, 0).wait()
        own_copy(h, 1).wait()
        return carry

    lax.fori_loop(0, KVH, own_wait, 0)
    pl.semaphore_wait(barrier, SEQ + GRP - 2)

    ex_q = Exchange("seq", SEQ, seq, lambda p: qmsg, qall, qss, qrs)
    ex_p = Exchange("seq", SEQ, seq, lambda p: pmsg.at[p], part, pss, prsem)
    ex_a = Exchange("grp", GRP, group, lambda p: amsg, aall, ass, ars)
    ex_o = Exchange("seq", SEQ, seq, lambda p: pblk.at[p // 2], prs, oss, ors)
    ex_r = Exchange("seq", 4, y, lambda p: rmsg, rall, rss, rrs, lambda p: 2 * p + z)
    ex_g = Exchange("grp", GRP, group, lambda p: gmsg.at[p], grs, gss, grsem)
    ex_h = Exchange("grp", GRP, group, lambda p: hmsg, hall, hss, hrs)
    ex_d = Exchange("seq", SEQ, seq, lambda p: dblk.at[p // 2], drs, dss, drsem)

    def relay(h, slot, shard, dst):
        return remote(kvg.at[shard, h], kvg.at[shard, h], kss.at[h, slot], krs.at[shard, h], {"seq": dst})

    turn = ((y + 1) // 2 + 1) % 2
    cross = 2 * (1 - y % 2) + z
    far = (seq + 4) % SEQ

    def sends(h):
        return [
            (0, seq, pair, y >= 0),
            (1, seq, up, y < 3),
            (2, seq, down, (y == 0) | ((y == 1) & (h % 2 == 1))),
            (3, pair, up, y < 3),
            (4, pair, down, y == 0),
            (5, cross, (seq + 2 + 4 * turn) % SEQ, h % 2 == turn),
            (6, far, pair, y >= 2),
        ]

    def start(h, slots):
        for slot, shard, dst, on in sends(h):
            if slot in slots:

                @pl.when(on)
                def _():
                    relay(h, slot, shard, dst).start()

    def arrived(h, shard):
        relay(h, 0, shard, pair).wait_recv()

    def relay_pair(h):
        start(h, (0,))

    def relay_own(h):
        start(h, (1, 2))

    def relay_other(h):
        arrived(h, pair)
        start(h, (3, 4))

    def relay_cross(h):
        @pl.when(h % 2 == turn)
        def _():
            arrived(h, cross)

        start(h, (5,))

    def relay_far(h):
        @pl.when(y >= 2)
        def _():
            arrived(h, far)

        start(h, (6,))

    def relay_last(h):
        for t in range(SEQ):
            seen = ((t == cross) & (h % 2 == turn)) | ((t == far) & (y >= 2))

            @pl.when((t // 2 < y) & jnp.logical_not(seen))
            def _():
                arrived(h, t)

    def relay_sent(h):
        for slot, shard, dst, on in sends(h):

            @pl.when(on)
            def _():
                relay(h, slot, shard, dst).wait_send()

    def dec0():
        ex_q.start()

    def dec1():
        ex_q.wait()
        start_c = jnp.sum(jnp.where(pick, starts, 0), axis=1, keepdims=True)
        len_c = jnp.sum(jnp.where(pick, lengths, 0), axis=1, keepdims=True)
        pos = seq * ROWS + iota((REQS, ROWS), 1)
        allowed = (pos >= start_c) & (pos < start_c + len_c)
        for t in range(SEQ):
            s = lax.dot_general(qall[t], kvg[seq, t, 0], NT, preferred_element_type=F32) * SCALE
            s = jnp.where(allowed, s, NEGATIVE)
            m = jnp.max(s, axis=1, keepdims=True)
            p = jnp.where(allowed, jnp.exp(s - m), 0.0)
            l = jnp.sum(p, axis=1, keepdims=True)
            pmsg[t, 0] = jnp.dot(p.astype(BF16), kvg[seq, t, 1], preferred_element_type=F32)
            pmsg[t, 1] = jnp.where(iota((REQS, HD), 1) == 0, m, l)
        part[seq] = pmsg[seq]
        ex_p.start()

    def dec2():
        ex_p.wait()
        key_row = jnp.dot(pick32, kn_ref[...], preferred_element_type=F32)
        value_row = jnp.dot(pick32, vn_ref[...], preferred_element_type=F32)
        own = jnp.sum(qmsg[...].astype(F32) * key_row, axis=1, keepdims=True) * SCALE
        top = own
        for t in range(SEQ):
            top = jnp.maximum(top, part[t, 1][:, 0:1])
        weight = jnp.exp(own - top)
        total = weight
        mixed = weight.astype(BF16).astype(F32) * value_row
        for t in range(SEQ):
            scale = jnp.exp(part[t, 1][:, 0:1] - top)
            total = total + scale * part[t, 1][:, 1:2]
            mixed = mixed + scale * part[t, 0]
        out = (mixed / total).astype(BF16)
        amsg[...] = out
        aall[group] = out
        ex_a.start()

    def dec3():
        ex_a.wait()
        rank_col = as_column(ranks, REQS)
        grp_col = as_column(groups, REQS)
        target = jnp.concatenate([grp_col * 32 + a * 4 + rank_col for a in range(GROUPED)], 0)
        gather = jnp.where(iota((256, 512), 1) == target, 1.0, 0.0).astype(BF16)
        rows = jnp.dot(gather, aall[...].reshape(512, HD), preferred_element_type=F32).astype(BF16)
        att = jnp.concatenate([rows[a * 32 : (a + 1) * 32] for a in range(GROUPED)], 1)
        weight_wait(0)
        proj = jnp.dot(att, owb[...], preferred_element_type=F32)
        for b in range(4):
            pblk[b] = proj[:, b * 128 : (b + 1) * 128]
        prs[seq] = pblk[y]
        ex_o.start()

    def dec4():
        ex_o.wait()
        r = hid_ref[:, pl.ds(pl.multiple_of(y * 128, 128), 128)].astype(F32)
        for t in range(SEQ):
            r = r + prs[t]
        rmsg[...] = r
        rall[y] = r
        ex_r.start()

    def dec5():
        ex_r.wait()
        r = jnp.concatenate([rall[b] for b in range(4)], 1)
        squares = jnp.sum(r * r, axis=1, keepdims=True)
        x = (r * gain_ref[...].astype(F32).reshape(1, -1)).astype(BF16)
        eye = iota((REQS, 128), 0) == iota((REQS, 128), 1)
        row = jnp.sum(jnp.where(eye, squares, 0.0), axis=0, keepdims=True)
        weight_wait(1)
        weight_wait(2)
        gate = jnp.dot(x, gwb[...], preferred_element_type=F32)
        upper = jnp.dot(x, uwb[...], preferred_element_type=F32)
        for t in range(GRP):
            gmsg[t, 0:32] = gate[:, t * 128 : (t + 1) * 128]
            gmsg[t, 32:64] = upper[:, t * 128 : (t + 1) * 128]
            gmsg[t, 64:72] = jnp.broadcast_to(row, (8, 128))
        grs[group] = gmsg[group]
        ex_g.start()

    def dec6():
        ex_g.wait()
        acc = grs[0]
        for t in range(1, GRP):
            acc = acc + grs[t]
        squares = as_column(acc[64:65, :], REQS)
        r = lax.rsqrt(squares / D + 1e-05)
        gate = acc[0:32] * r
        upper = acc[32:64] * r
        out = (gate / (1.0 + jnp.exp(-gate)) * upper).astype(BF16)
        hmsg[...] = out
        hall[group] = out
        ex_h.start()

    def dec7():
        ex_h.wait()
        hidden = jnp.concatenate([hall[t] for t in range(GRP)], 1)
        weight_wait(3)
        out = jnp.dot(hidden, dwb[...], preferred_element_type=F32)
        for b in range(4):
            dblk[b] = out[:, b * 128 : (b + 1) * 128]
        drs[seq] = dblk[y]
        ex_d.start()

    def dec8():
        ex_d.wait()
        out = rmsg[...]
        for t in range(SEQ):
            out = out + drs[t]
        dec_ref[...] = jnp.where(z == 0, out[:, 0:64], out[:, 64:128]).astype(BF16)

    steps = [dec0, dec1, dec2, dec3, dec4, dec5, dec6, dec7, dec8]

    def products(h, keys, first):
        count = keys.shape[0]
        keys = jnp.concatenate([keys, kx[pl.ds(pl.multiple_of(first * ROWS, ROWS), count), :]], 1)
        scores = []
        for a in range(GROUPED):
            cols = pl.ds(pl.multiple_of((h * GROUPED + a) * HD, HD), HD)
            queries = jnp.concatenate([qb[:, cols], qx[...]], 1)
            scores.append(lax.dot_general(queries, keys, NT, preferred_element_type=F32))
        return scores

    def folded(parts, op):
        return functools.reduce(op, [parts[:, i : i + 128] for i in range(0, parts.shape[1], 128)])

    def weigh(s, new):
        shift = new * (SCALE * LOG2E)
        return jnp.concatenate(
            [jnp.exp2(s[:, i : i + 128] * (SCALE * LOG2E) - shift) for i in range(0, s.shape[1], 128)], 1
        )

    def diagonal(h):
        q_copy(h).wait()
        values = kvg[seq, h, 1]
        causal = iota((ROWS, ROWS), 1) <= iota((ROWS, ROWS), 0)
        scores = products(h, kvg[seq, h, 0], seq)
        for a in range(GROUPED):
            s = jnp.where(causal, scores[a], NEGATIVE)
            new = jnp.max(folded(s, jnp.maximum), axis=1, keepdims=True)
            new = jnp.broadcast_to(new, (ROWS, 128))
            p = weigh(s, new)
            total[h, a] = folded(p, jnp.add)
            top[h, a] = new
            accum[h, a] = jnp.dot(p.astype(BF16), values, preferred_element_type=F32)

    def block(h, keys, values, first):
        scores = products(h, keys, first)
        for a in range(GROUPED):
            s = scores[a]
            old = top[h, a]
            new = jnp.maximum(old, jnp.max(folded(s, jnp.maximum), axis=1, keepdims=True))
            decay = jnp.exp2((old - new) * (SCALE * LOG2E))
            p = weigh(s, new)
            total[h, a] = total[h, a] * decay + folded(p, jnp.add)
            top[h, a] = new
            accum[h, a] = accum[h, a] * decay + jnp.dot(p.astype(BF16), values, preferred_element_type=F32)

    def when_head(h, action):
        @pl.when(h < KVH)
        def _():
            action(h)

    def middle(h):
        when_head(h + 1, relay_far)
        when_head(h + 2, relay_cross)
        when_head(h + 2, relay_other)
        when_head(h + 4, relay_own)
        when_head(h + 5, relay_pair)

    def rest(h):
        def each(j, carry):
            @pl.when(j == y // 2)
            def _():
                middle(h)

            keys = kvg[pl.ds(2 * j, 2), h, 0].reshape(512, HD)
            values = kvg[pl.ds(2 * j, 2), h, 1].reshape(512, HD)
            block(h, keys, values, 2 * j)
            return carry

        @pl.when(z == 1)
        def _():
            block(h, kvg[pair, h, 0], kvg[pair, h, 1], pair)

        lax.fori_loop(0, y, each, 0)

        @pl.when(y == 0)
        def _():
            middle(h)

        @pl.when(h >= 2)
        def _():
            out_copy(h).wait()

        for a in range(GROUPED):
            t = jnp.sum(total[h, a], axis=1, keepdims=True)
            ok = live[...] > 0.0
            ob[h % 2, :, a * HD : (a + 1) * HD] = jnp.where(ok, accum[h, a] / t, 0.0).astype(BF16)
        out_copy(h).start()

    relay_pair(0)
    relay_own(0)
    dec0()
    relay_pair(1)
    relay_own(1)
    opening = {
        2: [(relay_cross, 0), (relay_other, 0), (relay_own, 2), (relay_pair, 2)],
        3: [(dec1, None)],
        5: [(relay_far, 0), (relay_pair, 3)],
        6: [(relay_cross, 1), (relay_other, 1), (relay_own, 3), (relay_pair, 4)],
        7: [(dec2, None)],
    }

    def open_head(i, carry):
        diagonal(i)
        for k, actions in opening.items():

            @pl.when(i == k)
            def _():
                for action, head in actions:
                    action() if head is None else action(head)

        return carry

    lax.fori_loop(0, KVH, open_head, 0)

    def close_head(h, carry):
        relay_last(h)
        rest(h)
        for k, dec in enumerate(steps[3:]):
            pl.when(h == k)(dec)
        return carry

    lax.fori_loop(0, KVH, close_head, 0)

    def drain(h, carry):
        relay_sent(h)
        return carry

    lax.fori_loop(0, KVH, drain, 0)
    out_copy(KVH - 2).wait()
    out_copy(KVH - 1).wait()


def step(*operands):
    vmem = pl.BlockSpec(memory_space=pltpu.VMEM)
    hbm = pl.BlockSpec(memory_space=pl.ANY)
    dma = pltpu.SemaphoreType.DMA
    return pl.pallas_call(
        step_kernel,
        out_shape=(
            jax.ShapeDtypeStruct((ROWS, D), BF16),
            jax.ShapeDtypeStruct((REQS, 64), BF16),
        ),
        in_specs=[hbm] * 14,
        out_specs=(hbm, vmem),
        scratch_shapes=[
            pltpu.VMEM((32,), jnp.int32),
            pltpu.VMEM((32,), jnp.int32),
            pltpu.VMEM((32, 1024), BF16),
            pltpu.VMEM((32, 128), BF16),
            pltpu.VMEM((32, 128), BF16),
            pltpu.VMEM((32, 512), BF16),
            pltpu.VMEM((512,), BF16),
            pltpu.VMEM((SEQ, KVH, 2, ROWS, HD), BF16),
            pltpu.VMEM((ROWS, D), BF16),
            pltpu.VMEM((2, ROWS, 1024), BF16),
            pltpu.VMEM((ROWS, 128), BF16),
            pltpu.VMEM((SEQ * ROWS, 128), BF16),
            pltpu.VMEM((ROWS, 128), F32),
            pltpu.VMEM((KVH, GROUPED, ROWS, 128), F32),
            pltpu.VMEM((KVH, GROUPED, ROWS, 128), F32),
            pltpu.VMEM((KVH, GROUPED, ROWS, 128), F32),
            pltpu.VMEM((1024, 512), BF16),
            pltpu.VMEM((512, 2048), BF16),
            pltpu.VMEM((512, 2048), BF16),
            pltpu.VMEM((2048, 512), BF16),
            pltpu.VMEM((32, 128), BF16),
            pltpu.VMEM((8, 32, 128), BF16),
            pltpu.VMEM((8, 2, 32, 128), F32),
            pltpu.VMEM((8, 2, 32, 128), F32),
            pltpu.VMEM((32, 128), BF16),
            pltpu.VMEM((16, 32, 128), BF16),
            pltpu.VMEM((4, 32, 128), F32),
            pltpu.VMEM((8, 32, 128), F32),
            pltpu.VMEM((32, 128), F32),
            pltpu.VMEM((4, 32, 128), F32),
            pltpu.VMEM((16, 72, 128), F32),
            pltpu.VMEM((16, 72, 128), F32),
            pltpu.VMEM((32, 128), BF16),
            pltpu.VMEM((16, 32, 128), BF16),
            pltpu.VMEM((4, 32, 128), F32),
            pltpu.VMEM((8, 32, 128), F32),
            dma((7,)),
            dma((4,)),
            dma((8, 2)),
            dma((8,)),
            dma((2,)),
            dma((8, 7)),
            dma((8, 8)),
        ]
        + [dma((8,))] * 4
        + [dma((16,))] * 2
        + [dma((8,))] * 2
        + [dma((4,))] * 2
        + [dma((16,))] * 4
        + [dma((8,))] * 2,
        compiler_params=pltpu.CompilerParams(collective_id=0, has_side_effects=True, vmem_limit_bytes=58 << 20),
        name="step",
    )(*operands)


def hand_over_kernel(att_ref, dec_ref, att_out, dec_out, att_buf, dec_buf, read_sems, write_sems):
    reads = [pltpu.make_async_copy(dec_ref, dec_buf, read_sems.at[8])]
    writes = [pltpu.make_async_copy(dec_buf, dec_out, write_sems.at[8])]
    for i in range(8):
        rows = pl.ds(i * 32, 32)
        reads.append(pltpu.make_async_copy(att_ref.at[rows], att_buf.at[rows], read_sems.at[i]))
        writes.append(pltpu.make_async_copy(att_buf.at[rows], att_out.at[rows], write_sems.at[i]))
    for read in reads:
        read.start()
    for read, write in zip(reads, writes):
        read.wait()
        write.start()
    for write in writes:
        write.wait()


def hand_over(attention, decode_hidden):
    hbm = pl.BlockSpec(memory_space=pl.ANY)
    return pl.pallas_call(
        hand_over_kernel,
        out_shape=(
            jax.ShapeDtypeStruct(attention.shape, BF16),
            jax.ShapeDtypeStruct(decode_hidden.shape, BF16),
        ),
        in_specs=[hbm] * 2,
        out_specs=(hbm, hbm),
        scratch_shapes=[
            pltpu.VMEM(attention.shape, BF16),
            pltpu.VMEM(decode_hidden.shape, BF16),
            pltpu.SemaphoreType.DMA((9,)),
            pltpu.SemaphoreType.DMA((9,)),
        ],
        compiler_params=pltpu.CompilerParams(vmem_limit_bytes=60 << 20),
        name="hand_over",
    )(attention, decode_hidden)


def shards(
    lengths, group_of, query_pre, key_pre, value_pre, query_new, key_new, value_new,
    hidden_new, out_weight, norm_gain, gate_weight, up_weight, down_weight,
):
    attention, decode_hidden = step(
        lengths, group_of, query_new, key_new, value_new, hidden_new,
        norm_gain, out_weight, gate_weight, up_weight, down_weight, query_pre, key_pre, value_pre,
    )
    return hand_over(attention, decode_hidden)


def solution(mesh):
    both = P(("grp", "seq"), None)
    return jax.shard_map(
        shards,
        mesh=mesh,
        in_specs=(
            P(), P(), both, both, both, P(None, "seq"), P(None, "seq"), P(None, "seq"), P(None, "grp"),
            P("seq", "grp"), P("grp"), P("grp", "seq"), P("grp", "seq"), P("seq", "grp"),
        ),
        out_specs=(both, P(None, ("grp", "seq"))),
        check_vma=False,
    )
```
